128 devices in a mesh: gx: 16 (over y, z), gy: 8 (over x, core).
Axes of the slice: x: 4, y: 4, z: 4, core: 2. Of those that a mesh axis runs over, the one named last changes fastest.
Arguments:
- features: bfloat16 [2048, 512, 128], P('gx', 'gy'), may hold values from -6 to 6
- cotangent: bfloat16 [2048, 512, 128], P('gx', 'gy'), may hold values from -31 to 31
- kernel: float32 [7, 7, 128], replicated, may hold values from -0.875 to 0.875
- kernel_bias: float32 [128], replicated, may hold values from -3 to 3
- norm_gain: float32 [128], replicated, may hold values from 0.1 to 1.9
- norm_shift: float32 [128], replicated, may hold values from -3 to 3
- w_up: bfloat16 [128, 512], replicated, may hold values from -0.5 to 0.5
- b_up: float32 [512], replicated, may hold values from -3 to 3
- w_down: bfloat16 [512, 128], replicated, may hold values from -0.25 to 0.25
- b_down: float32 [128], replicated, may hold values from -3 to 3
- layer_scale: float32 [128], replicated, may hold values from 0.3 to 3
Outputs:
- d_features: bfloat16 [2048, 512, 128], P('gx', 'gy')
- d_kernel: float32 [7, 7, 128], replicated
- d_kernel_bias: float32 [128], replicated
- d_norm_gain: float32 [128], replicated
- d_norm_shift: float32 [128], replicated
- d_w_up: float32 [128, 512], replicated
- d_b_up: float32 [512], replicated
- d_w_down: float32 [512, 128], replicated
- d_b_down: float32 [128], replicated
- d_layer_scale: float32 [128], replicated
The draws below stay inside these ranges and needn't reach their ends.
All inputs are finite; a program needn't handle non-finite values.
Results may differ from the reference program's by a relative error of at most 0.0072.
Values may be sent and summed in bfloat16 or wider, within the bound.
No kernel may reach another device: no remote copies, remote signals or barrier semaphores. Data moves between devices by JAX's collectives and lax.ppermute only.
A program may use at most 64 MiB of HBM per device.

```python
import math
import jax
import jax.numpy as jnp
from jax import lax

C = 128
E = 512
TAPS = 7
NH = 2048
NW = 512


def draw_cotangent(key, part):
    key_base = jax.random.fold_in(key, 11)
    key_rough = jax.random.fold_in(key, 23)
    base_values = jnp.clip(jax.random.normal(key_base, (NH, NW, C), jnp.float32), -5.0, 5.0)
    rough_factor = jnp.exp(jax.random.uniform(key_rough, (NH, NW, 1), jnp.float32, -0.7, 0.7))
    ramp_factor = 1.0 + 2.0 * jnp.arange(NH, dtype=jnp.float32) / NH
    return (base_values * rough_factor * ramp_factor[:, None, None]).astype(jnp.bfloat16)


def level_of(rng, shape, pieces, smallest, high):
    gain, own = 1.0, jax.random.fold_in(rng, 6)
    for axis_at, blocks in pieces:
        draws = jnp.exp(jax.random.uniform(jax.random.fold_in(own, axis_at), (blocks,), jnp.float32, smallest / len(pieces), high / len(pieces)))
        gain = gain * jnp.repeat(draws, shape[axis_at] // blocks).reshape([-1 if axis == axis_at else 1 for axis in range(len(shape))])
    return gain


def scatter_about(key, dims, deviation, reach, cuts=(), kind=jnp.bfloat16):
    values = jax.random.normal(key, dims, jnp.float32) * deviation
    if len(cuts) > 0:
        values = level_of(key, dims, cuts, -0.22, 0.18) * values
    return jnp.clip(values, min=-reach, max=reach).astype(kind)


def setup_inputs(seed: int = 0) -> dict:
    seeds = jax.random.split(jax.random.key(seed), 12)
    features = scatter_about(seeds[0], (NH, NW, C), 1.0, 6.0, ((0, 16), (1, 8)))
    cotangent = draw_cotangent(jax.random.fold_in(seeds[11], 71), 0)
    kernel = scatter_about(seeds[2], (TAPS, TAPS, C), (TAPS * TAPS) ** -0.5, 0.875, (), jnp.float32)
    kernel_bias = scatter_about(seeds[3], (C,), 0.5, 3.0, (), jnp.float32)
    norm_gain = jnp.clip(1.0 + 0.18 * jax.random.normal(seeds[4], (C,), jnp.float32), 0.1, 1.9)
    norm_shift = scatter_about(seeds[5], (C,), 0.5, 3.0, (), jnp.float32)
    w_up = scatter_about(seeds[6], (C, E), C ** -0.5, 0.5)
    b_up = scatter_about(seeds[7], (E,), 0.5, 3.0, (), jnp.float32)
    w_down = scatter_about(seeds[8], (E, C), E ** -0.5, 0.25)
    b_down = scatter_about(seeds[9], (C,), 0.5, 3.0, (), jnp.float32)
    layer_scale = jnp.clip(jnp.exp(jax.random.uniform(seeds[10], (C,), jnp.float32, math.log(0.3), math.log(3.0))), 0.3, 3.0)
    return dict(features=features, cotangent=cotangent, kernel=kernel, kernel_bias=kernel_bias, norm_gain=norm_gain, norm_shift=norm_shift, w_up=w_up, b_up=b_up, w_down=w_down, b_down=b_down, layer_scale=layer_scale)


EPSILON = 1e-06

def gelu_pair(hidden):
    erf_part = jax.scipy.special.erf(hidden * 0.7071067811865476)
    value = 0.5 * hidden * (1.0 + erf_part)
    slope_value = 0.5 * (1.0 + erf_part) + hidden * jnp.exp(-0.5 * hidden * hidden) * 0.3989422804014327
    return (value, slope_value)

def product(spec, left, right):
    return jnp.einsum(spec, left.astype(jnp.float32), right.astype(jnp.float32))

def depthwise(padded, kernel, row_count, col_count):
    tap_count = kernel.shape[0]
    accum = jnp.zeros((row_count, col_count, kernel.shape[2]), jnp.float32)
    for row_tap in range(tap_count):
        for col_tap in range(tap_count):
            window = padded[row_tap:row_tap + row_count, col_tap:col_tap + col_count]
            accum = accum + window.astype(jnp.float32) * kernel[row_tap, col_tap]
    return accum

def spread_back(padded, kernel, row_count, col_count):
    tap_count = kernel.shape[0]
    edge_cells = tap_count - 1
    accum = jnp.zeros((row_count, col_count, kernel.shape[2]), jnp.float32)
    for row_tap in range(tap_count):
        for col_tap in range(tap_count):
            window = padded[edge_cells - row_tap:edge_cells - row_tap + row_count, edge_cells - col_tap:edge_cells - col_tap + col_count]
            accum = accum + window * kernel[row_tap, col_tap]
    return accum

def kernel_grad(slopes_in, padded, tap_count):
    row_count, col_count = (slopes_in.shape[0], slopes_in.shape[1])
    rows_out = []
    for row_tap in range(tap_count):
        line = []
        for col_tap in range(tap_count):
            window = padded[row_tap:row_tap + row_count, col_tap:col_tap + col_count].astype(jnp.float32)
            line.append(lax.optimization_barrier(jnp.sum(slopes_in * window, axis=(0, 1))))
        rows_out.append(jnp.stack(line, 0))
    return jnp.stack(rows_out, 0)

def layer_back(conv_out, cotan, norm_gain, norm_shift, w_up, b_up, w_down, b_down, layer_scale, row_lo, row_hi, col_lo, col_hi):
    chan_mean = lax.optimization_barrier(jnp.mean(conv_out, axis=-1, keepdims=True))
    centred = conv_out - chan_mean
    inv_std = lax.rsqrt(lax.optimization_barrier(jnp.mean(centred * centred, axis=-1, keepdims=True)) + EPSILON)
    normed = centred * inv_std
    normal_out = (normed * norm_gain + norm_shift).astype(jnp.bfloat16)
    hidden = product('rwc,ce->rwe', normal_out, w_up) + b_up
    active, gelu_slope = gelu_pair(hidden)
    active = active.astype(jnp.bfloat16)
    output = product('rwe,ec->rwc', active, w_down) + b_down
    cot_float = cotan.astype(jnp.float32)
    d_output = (cot_float * layer_scale).astype(jnp.bfloat16)
    d_active = product('rwc,ec->rwe', d_output, w_down)
    d_hidden = (d_active * gelu_slope).astype(jnp.bfloat16)
    d_normal = product('rwe,ce->rwc', d_hidden, w_up)
    d_normed = d_normal * norm_gain
    first_mean = lax.optimization_barrier(jnp.mean(d_normed, axis=-1, keepdims=True))
    second_mean = lax.optimization_barrier(jnp.mean(d_normed * normed, axis=-1, keepdims=True))
    d_conv = inv_std * (d_normed - first_mean - normed * second_mean)
    rsel = slice(row_lo, row_hi)
    csel = slice(col_lo, col_hi)
    d_gain = lax.optimization_barrier(jnp.sum((d_normal * normed)[rsel, csel], axis=(0, 1)))
    d_shift = lax.optimization_barrier(jnp.sum(d_normal[rsel, csel], axis=(0, 1)))
    d_wup = product('rwc,rwe->ce', normal_out[rsel, csel], d_hidden[rsel, csel])
    d_bup = lax.optimization_barrier(jnp.sum(d_hidden[rsel, csel].astype(jnp.float32), axis=(0, 1)))
    d_wdown = product('rwe,rwc->ec', active[rsel, csel], d_output[rsel, csel])
    d_bdown = lax.optimization_barrier(jnp.sum(d_output[rsel, csel].astype(jnp.float32), axis=(0, 1)))
    d_lscale = lax.optimization_barrier(jnp.sum((cot_float * output)[rsel, csel], axis=(0, 1)))
    return (d_conv, (d_gain, d_shift, d_wup, d_bup, d_wdown, d_bdown, d_lscale))

def reference(features, cotangent, kernel, kernel_bias, norm_gain, norm_shift, w_up, b_up, w_down, b_down, layer_scale):
    tap_count = kernel.shape[0]
    reach_cells = tap_count // 2
    deep = 2 * reach_cells
    wrapped_x = jnp.concatenate([features[NH - deep:], features, features[:deep]], axis=0)
    padded_x = jnp.pad(wrapped_x, ((0, 0), (deep, deep), (0, 0)))
    wrapped_c = jnp.concatenate([cotangent[NH - reach_cells:], cotangent, cotangent[:reach_cells]], axis=0)
    padded_c = jnp.pad(wrapped_c, ((0, 0), (reach_cells, reach_cells), (0, 0)))
    block_rows = math.gcd(NH, 128)
    block_count = NH // block_rows
    col_place = lax.iota(jnp.int32, NW + 2 * reach_cells) - reach_cells
    keep_mask = (col_place >= 0) & (col_place < NW)

    def step(running, block_index):
        row_start = (block_index * block_rows).astype(jnp.int32)
        zero_index = jnp.zeros((), jnp.int32)
        x_block = lax.dynamic_slice(padded_x, (row_start, zero_index, zero_index), (block_rows + 2 * deep, NW + 2 * deep, C))
        c_block = lax.dynamic_slice(padded_c, (row_start, zero_index, zero_index), (block_rows + deep, NW + deep, C))
        conv_out = depthwise(x_block, kernel, block_rows + deep, NW + deep) + kernel_bias
        d_conv, layer_grads = layer_back(conv_out, c_block, norm_gain, norm_shift, w_up, b_up, w_down, b_down, layer_scale, reach_cells, reach_cells + block_rows, reach_cells, reach_cells + NW)
        d_conv = jnp.where(keep_mask[None, :, None], d_conv, 0.0)
        inner_slope = d_conv[reach_cells:reach_cells + block_rows, reach_cells:reach_cells + NW]
        inner_x = x_block[reach_cells:reach_cells + block_rows + deep, reach_cells:reach_cells + NW + deep]
        d_kern = kernel_grad(inner_slope, inner_x, tap_count)
        d_kbias = lax.optimization_barrier(jnp.sum(inner_slope, axis=(0, 1)))
        spread = spread_back(d_conv, kernel, block_rows, NW)
        own_cot = c_block[reach_cells:reach_cells + block_rows, reach_cells:reach_cells + NW].astype(jnp.float32)
        d_block = (own_cot + spread).astype(jnp.bfloat16)
        fresh = (d_kern, d_kbias) + layer_grads
        updated = tuple((old + new for old, new in zip(running, fresh)))
        return (updated, d_block)
    initial = (jnp.zeros((tap_count, tap_count, C), jnp.float32), jnp.zeros((C,), jnp.float32), jnp.zeros((C,), jnp.float32), jnp.zeros((C,), jnp.float32), jnp.zeros((C, E), jnp.float32), jnp.zeros((E,), jnp.float32), jnp.zeros((E, C), jnp.float32), jnp.zeros((C,), jnp.float32), jnp.zeros((C,), jnp.float32))
    sums, blocks = lax.scan(step, initial, jnp.arange(block_count, dtype=jnp.int32))
    d_features = blocks.reshape(NH, NW, C)
    factor = 1.0 / math.sqrt(NH * NW)
    d_kern, d_kbias, d_gain, d_shift, d_wup, d_bup, d_wdown, d_bdown, d_lscale = sums
    return (d_features, d_kern * factor, d_kbias * factor, d_gain * factor, d_shift * factor, d_wup * factor, d_bup * factor, d_wdown * factor, d_bdown * factor, d_lscale * factor)
```

```python
import functools
import math

import jax
import jax.numpy as jnp
from jax import lax
from jax.experimental import pallas as pl
from jax.experimental.pallas import tpu as pltpu
from jax.sharding import PartitionSpec as P

EPSILON = 1e-06
REACH = 3
TAPS = 7
PAIRS = 4
OFF = 8
GRANT = 58 * 2**20


def shifted(cells, axis, step, cyclic):
    count = lax.axis_size(axis)
    pairs = [(i, (i + step) % count) for i in range(count) if cyclic or 0 <= i + step < count]
    return lax.ppermute(cells, axis, pairs)


def halo(cells):
    rows, cols = cells.shape[0], cells.shape[1]
    top = shifted(cells[rows - REACH :], "gx", 1, True)
    bottom = shifted(cells[:REACH], "gx", -1, True)

    def edge(start):
        cut = [part[:, start : start + REACH] for part in (top, cells, bottom)]
        return jnp.concatenate(cut, axis=0)

    left = shifted(edge(cols - REACH), "gy", 1, False)
    right = shifted(edge(0), "gy", -1, False)
    return top, bottom, left, right


def fill_padded(own, top, bottom, left, right, pad_ref):
    rows, cols = own.shape[0], own.shape[1]
    inner = pl.ds(OFF, cols)
    pad_ref[0:REACH, inner, :] = top[...].astype(jnp.float32)
    pad_ref[REACH + rows : 2 * REACH + rows, inner, :] = bottom[...].astype(jnp.float32)

    def body(r, carry):
        pad_ref[REACH + r, inner, :] = own[r].astype(jnp.float32)
        return carry

    lax.fori_loop(0, rows, body, 0, unroll=4)

    def sides(r, carry):
        pad_ref[r, OFF - REACH : OFF, :] = left[r].astype(jnp.float32)
        pad_ref[r, OFF + cols : OFF + cols + REACH, :] = right[r].astype(jnp.float32)
        return carry

    lax.fori_loop(0, rows + 2 * REACH, sides, 0, unroll=2)


def fill_pairs(pad_ref, pair_ref):
    half = pair_ref.shape[1] // pad_ref.shape[0]

    def body(r, carry):
        for m in range(PAIRS):
            for p in range(2):
                start = OFF - REACH + 2 * m + p
                cells = pad_ref[r, pl.ds(start, half, stride=2), :]
                pair_ref[m, pl.ds(pl.multiple_of(r * half, half), half), p * 128 : p * 128 + 128] = (
                    cells.astype(jnp.bfloat16)
                )
        return carry

    lax.fori_loop(0, pad_ref.shape[0], body, 0, unroll=2)


def fill_weights(kern_ref, w_ref, flip):
    width = kern_ref.shape[2]
    row = lax.broadcasted_iota(jnp.int32, (width, width), 0)
    col = lax.broadcasted_iota(jnp.int32, (width, width), 1)
    eye = row == col
    for a in range(TAPS):
        for m in range(PAIRS):
            for p in range(2):
                for q in range(2):
                    b = 2 * m + p - q
                    base = ((a * PAIRS + m) * 2 + p) * width
                    if 0 <= b < TAPS:
                        tap = (
                            kern_ref[TAPS - 1 - a, pl.ds(TAPS - 1 - b, 1), :]
                            if flip
                            else kern_ref[a, pl.ds(b, 1), :]
                        )
                        block = jnp.where(eye, jnp.broadcast_to(tap, (width, width)), 0.0)
                    else:
                        block = jnp.zeros((width, width), jnp.float32)
                    w_ref[base : base + width, q * width : (q + 1) * width] = block.astype(
                        jnp.bfloat16
                    )


def conv_pairs(pair_ref, w_ref, row0, row_count, half):
    lhs = jnp.concatenate(
        [
            pair_ref[m, pl.ds(pl.multiple_of((row0 + a) * half, half), row_count * half), :]
            for a in range(TAPS)
            for m in range(PAIRS)
        ],
        axis=1,
    )
    return jnp.dot(lhs, w_ref[...], preferred_element_type=jnp.float32)


def dot(left, right, dims):
    return lax.dot_general(left, right, (dims, ((), ())), preferred_element_type=jnp.float32)


def fold(values):
    return jnp.sum(values.reshape(-1, 8, values.shape[-1]), axis=0)


def layer_kernel(
    block_rows,
    own,
    top,
    bottom,
    left,
    right,
    cot_ref,
    kern_ref,
    kbias_ref,
    gain_ref,
    shift_ref,
    wup_ref,
    bup_ref,
    wdown_ref,
    scale_ref,
    dconv_ref,
    dwup_ref,
    dgt_ref,
    sums_ref,
    dbup_ref,
    pad_ref,
    pair_ref,
    w_ref,
    cell_ref,
):
    step = pl.program_id(0)
    half = own.shape[1] // 2
    count = block_rows * half

    @pl.when(step == 0)
    def _():
        fill_weights(kern_ref, w_ref, False)
        fill_padded(own, top, bottom, left, right, pad_ref)
        fill_pairs(pad_ref, pair_ref)
        dwup_ref[...] = jnp.zeros_like(dwup_ref)
        dgt_ref[...] = jnp.zeros_like(dgt_ref)
        sums_ref[...] = jnp.zeros_like(sums_ref)
        dbup_ref[...] = jnp.zeros_like(dbup_ref)

    conv = conv_pairs(pair_ref, w_ref, step * block_rows, block_rows, half)
    conv = jnp.concatenate([conv[:, :128], conv[:, 128:]], axis=0) + kbias_ref[...]
    gain = gain_ref[...]
    centred = conv - jnp.mean(conv, axis=-1, keepdims=True)
    inv_std = lax.rsqrt(jnp.mean(centred * centred, axis=-1, keepdims=True) + EPSILON)
    normed = centred * inv_std
    normal = (normed * gain + shift_ref[...]).astype(jnp.bfloat16)
    hidden = dot(normal, wup_ref[...], ((1,), (0,))) + bup_ref[...]
    cdf = 0.5 * (1.0 + lax.erf(hidden * 0.7071067811865476))
    active = (hidden * cdf).astype(jnp.bfloat16)
    slope = cdf + hidden * jnp.exp(-0.5 * hidden * hidden) * 0.3989422804014327
    cell_ref[...] = cot_ref[...].astype(jnp.float32)
    cot = jnp.concatenate([cell_ref[pl.ds(q, count, stride=2), :] for q in range(2)], axis=0)
    d_output = (cot * scale_ref[...]).astype(jnp.bfloat16)
    d_hidden = (dot(d_output, wdown_ref[...], ((1,), (1,))) * slope).astype(jnp.bfloat16)
    d_normal = dot(d_hidden, wup_ref[...], ((1,), (1,)))
    d_normed = d_normal * gain
    first = jnp.mean(d_normed, axis=-1, keepdims=True)
    second = jnp.mean(d_normed * normed, axis=-1, keepdims=True)
    d_conv = inv_std * (d_normed - first - normed * second)
    sums_ref[0] += fold(d_conv)
    sums_ref[1] += fold(d_normal * normed)
    sums_ref[2] += fold(d_normal)
    sums_ref[3] += fold(cot)
    dbup_ref[...] += fold(d_hidden.astype(jnp.float32))
    dwup_ref[...] += dot(normal, d_hidden, ((0,), (0,)))
    dgt_ref[...] += dot(cot.astype(jnp.bfloat16), active, ((0,), (0,)))
    for q in range(2):
        cell_ref[pl.ds(q, count, stride=2), :] = d_conv[q * count : (q + 1) * count]
    dconv_ref[...] = cell_ref[...].astype(jnp.bfloat16)


def layer(x, sides, cotangent, kernel, kbias, gain, shift, wup, bup, wdown, scale):
    rows, cols, width = x.shape
    hidden = wup.shape[1]
    block_rows = 8
    block = block_rows * cols
    whole = lambda a: pl.BlockSpec(a.shape, lambda i: (0,) * a.ndim)
    row = lambda a: a.reshape(1, -1)
    consts = (kernel, row(kbias), row(gain), row(shift), wup, row(bup), wdown, row(scale))
    padded = rows + 2 * REACH
    cells = pl.BlockSpec((block, width), lambda i: (i, 0))
    full = lambda *shape: pl.BlockSpec(shape, lambda i: (0,) * len(shape))
    f32 = jnp.float32
    return pl.pallas_call(
        functools.partial(layer_kernel, block_rows),
        grid=(rows // block_rows,),
        in_specs=[whole(x)]
        + [whole(s) for s in sides]
        + [cells]
        + [whole(c) for c in consts],
        out_specs=[
            cells,
            full(width, hidden),
            full(width, hidden),
            full(4, 8, width),
            full(8, hidden),
        ],
        out_shape=[
            jax.ShapeDtypeStruct((rows * cols, width), jnp.bfloat16),
            jax.ShapeDtypeStruct((width, hidden), f32),
            jax.ShapeDtypeStruct((width, hidden), f32),
            jax.ShapeDtypeStruct((4, 8, width), f32),
            jax.ShapeDtypeStruct((8, hidden), f32),
        ],
        scratch_shapes=[
            pltpu.VMEM((padded, cols + 2 * OFF, width), f32),
            pltpu.VMEM((PAIRS, padded * cols // 2, 2 * width), jnp.bfloat16),
            pltpu.VMEM((TAPS * PAIRS * 2 * width, 2 * width), jnp.bfloat16),
            pltpu.VMEM((block, width), f32),
        ],
        compiler_params=pltpu.CompilerParams(vmem_limit_bytes=GRANT),
        name="layer",
    )(x, *sides, cotangent.reshape(rows * cols, width), *consts)


def tap_kernel(own, top, bottom, left, right, dconv_ref, out_ref, pad_ref, grad_ref):
    rows, cols = own.shape[0], own.shape[1]
    edge = TAPS - 1
    fill_padded(own, top, bottom, left, right, pad_ref)
    grad_ref[0:edge] = jnp.zeros((edge,) + grad_ref.shape[1:], jnp.float32)
    grad_ref[edge + rows :] = jnp.zeros((edge,) + grad_ref.shape[1:], jnp.float32)

    def copy(r, carry):
        grad_ref[edge + r] = dconv_ref[pl.ds(pl.multiple_of(r * cols, cols), cols), :].astype(
            jnp.float32
        )
        return carry

    lax.fori_loop(0, rows, copy, 0, unroll=4)
    for b in range(TAPS):

        def body(i, sums):
            r = 2 * i
            sums = list(sums)
            for s in range(cols // 8):
                grads = [grad_ref[r + k, 8 * s : 8 * s + 8, :] for k in range(TAPS + 1)]
                start = OFF - REACH + b + 8 * s
                cells = [pad_ref[r + u, start : start + 8, :] for u in range(2)]
                for a in range(TAPS):
                    sums[a] = sums[a] + (
                        cells[0] * grads[edge - a] + cells[1] * grads[TAPS - a]
                    )
            return tuple(sums)

        zero = jnp.zeros((8, own.shape[2]), jnp.float32)
        sums = lax.fori_loop(0, (rows + edge) // 2, body, (zero,) * TAPS)
        for a in range(TAPS):
            out_ref[a, b] = sums[a]


def tap_grads(x, sides, dconv):
    rows, cols, width = x.shape
    padded = rows + 2 * REACH
    return pl.pallas_call(
        tap_kernel,
        out_shape=jax.ShapeDtypeStruct((TAPS, TAPS, 8, width), jnp.float32),
        scratch_shapes=[
            pltpu.VMEM((padded, cols + 2 * OFF, width), jnp.float32),
            pltpu.VMEM((rows + 2 * TAPS - 2, cols, width), jnp.float32),
        ],
        compiler_params=pltpu.CompilerParams(vmem_limit_bytes=GRANT),
        cost_estimate=pl.CostEstimate(
            flops=2 * TAPS * TAPS * x.size, bytes_accessed=4 * x.size, transcendentals=0
        ),
        name="taps",
    )(x, *sides, dconv)


def spread_kernel(
    block_rows, own, top, bottom, left, right, cot_ref, kern_ref, out_ref, pad_ref, pair_ref, w_ref, cell_ref
):
    step = pl.program_id(0)
    half = own.shape[1] // 2
    count = block_rows * half

    @pl.when(step == 0)
    def _():
        fill_weights(kern_ref, w_ref, True)
        fill_padded(own, top, bottom, left, right, pad_ref)
        fill_pairs(pad_ref, pair_ref)

    conv = conv_pairs(pair_ref, w_ref, step * block_rows, block_rows, half)
    for q in range(2):
        cell_ref[pl.ds(q, count, stride=2), :] = conv[:, q * 128 : q * 128 + 128]
    out_ref[...] = (cell_ref[...] + cot_ref[...].astype(jnp.float32)).astype(jnp.bfloat16)


def spread(dconv, sides, cotangent, kernel):
    rows, cols, width = dconv.shape
    block_rows = 16
    block = block_rows * cols
    padded = rows + 2 * REACH
    whole = lambda a: pl.BlockSpec(a.shape, lambda i: (0,) * a.ndim)
    cells = pl.BlockSpec((block, width), lambda i: (i, 0))
    return pl.pallas_call(
        functools.partial(spread_kernel, block_rows),
        grid=(rows // block_rows,),
        in_specs=[whole(dconv)] + [whole(s) for s in sides] + [cells, whole(kernel)],
        out_specs=cells,
        out_shape=jax.ShapeDtypeStruct((rows * cols, width), jnp.bfloat16),
        scratch_shapes=[
            pltpu.VMEM((padded, cols + 2 * OFF, width), jnp.float32),
            pltpu.VMEM((PAIRS, padded * cols // 2, 2 * width), jnp.bfloat16),
            pltpu.VMEM((TAPS * PAIRS * 2 * width, 2 * width), jnp.bfloat16),
            pltpu.VMEM((block, width), jnp.float32),
        ],
        compiler_params=pltpu.CompilerParams(vmem_limit_bytes=GRANT),
        name="spread",
    )(dconv, *sides, cotangent.reshape(rows * cols, width), kernel).reshape(rows, cols, width)


def total(parts):
    axes = ("gx", "gy")
    share = lax.all_to_all(parts, axes, split_axis=0, concat_axis=0, tiled=True)
    share = jnp.sum(share.astype(jnp.float32), axis=0).astype(parts.dtype)
    copies = jnp.broadcast_to(share[None], parts.shape)
    return lax.all_to_all(copies, axes, split_axis=0, concat_axis=0, tiled=True)


def local(
    features, cotangent, kernel, kernel_bias, norm_gain, norm_shift, w_up, b_up, w_down, b_down, layer_scale
):
    rows, cols, width = features.shape
    hidden = w_up.shape[1]
    devices = lax.axis_size("gx") * lax.axis_size("gy")
    x_sides = halo(features)
    dconv, d_wup, d_gt, sums, d_bup = layer(
        features, x_sides, cotangent, kernel, kernel_bias, norm_gain, norm_shift, w_up, b_up, w_down, layer_scale
    )
    d_sides = halo(dconv.reshape(rows, cols, width))
    d_kern = tap_grads(features, x_sides, dconv)
    d_features = spread(dconv.reshape(rows, cols, width), d_sides, cotangent, kernel)

    lanes = hidden // width
    small = jnp.concatenate(
        [
            jnp.sum(d_kern, axis=2).reshape(TAPS * TAPS, width),
            jnp.sum(sums, axis=1),
            jnp.sum(d_bup, axis=0).reshape(lanes, width),
        ],
        axis=0,
    )
    small = jnp.pad(small, ((0, devices - small.shape[0]), (0, 0)))
    parts = jnp.concatenate(
        [d_wup.reshape(width, lanes, width), d_gt.reshape(width, lanes, width), small[:, None]], axis=1
    )
    parts = jnp.pad(parts, ((0, 0), (0, 16 - parts.shape[1]), (0, 0))).astype(jnp.bfloat16)
    summed = total(parts).astype(jnp.float32)
    factor = 1.0 / math.sqrt(rows * cols * devices)
    summed = summed * factor
    g_wup = summed[:, :lanes].reshape(width, hidden)
    g_gt = summed[:, lanes : 2 * lanes].reshape(width, hidden)
    small = summed[:, 2 * lanes]
    taps = TAPS * TAPS
    cot_sum = small[taps + 3]
    g_lscale = jnp.sum(w_down.astype(jnp.float32).T * g_gt, axis=1) + b_down * cot_sum
    return (
        d_features,
        small[:taps].reshape(TAPS, TAPS, width),
        small[taps],
        small[taps + 1],
        small[taps + 2],
        g_wup,
        small[taps + 4 : taps + 4 + lanes].reshape(hidden),
        (g_gt * layer_scale[:, None]).T,
        layer_scale * cot_sum,
        g_lscale,
    )


def solution(mesh):
    placed = (P("gx", "gy", None), P("gx", "gy", None), P(), P(), P(), P(), P(), P(), P(), P(), P())
    return jax.shard_map(
        local,
        mesh=mesh,
        in_specs=placed,
        out_specs=(P("gx", "gy", None), P(), P(), P(), P(), P(), P(), P(), P(), P()),
        check_vma=False,
    )
```

```python
import functools
import math

import jax
import jax.numpy as jnp
from jax import lax
from jax.experimental import pallas as pl
from jax.experimental.pallas import tpu as pltpu
from jax.sharding import PartitionSpec as P

EPSILON = 1e-06
REACH = 3
TAPS = 7
PAIRS = 4
OFF = 8
GRANT = 58 * 2**20
LANES = 4
SHARE = 16


def shifted(cells, axis, step, cyclic):
    count = lax.axis_size(axis)
    pairs = [(i, (i + step) % count) for i in range(count) if cyclic or 0 <= i + step < count]
    return lax.ppermute(cells, axis, pairs)


def halo(cells):
    rows, cols = cells.shape[0], cells.shape[1]
    top = shifted(cells[rows - REACH :], "gx", 1, True)
    bottom = shifted(cells[:REACH], "gx", -1, True)

    def edge(start):
        cut = [part[:, start : start + REACH] for part in (top, cells, bottom)]
        return jnp.concatenate(cut, axis=0)

    left = shifted(edge(cols - REACH), "gy", 1, False)
    right = shifted(edge(0), "gy", -1, False)
    return top, bottom, left, right


def fill_padded(own, top, bottom, left, right, pad_ref):
    rows, cols = own.shape[0], own.shape[1]
    inner = pl.ds(OFF, cols)
    pad_ref[0:REACH, inner, :] = top[...].astype(jnp.float32)
    pad_ref[REACH + rows : 2 * REACH + rows, inner, :] = bottom[...].astype(jnp.float32)

    def body(r, carry):
        pad_ref[REACH + r, inner, :] = own[r].astype(jnp.float32)
        return carry

    lax.fori_loop(0, rows, body, 0, unroll=4)

    def sides(r, carry):
        pad_ref[r, OFF - REACH : OFF, :] = left[r].astype(jnp.float32)
        pad_ref[r, OFF + cols : OFF + cols + REACH, :] = right[r].astype(jnp.float32)
        return carry

    lax.fori_loop(0, rows + 2 * REACH, sides, 0, unroll=2)


def fill_pairs(pad_ref, pair_ref):
    half = pair_ref.shape[1] // pad_ref.shape[0]

    def body(r, carry):
        for m in range(PAIRS):
            for p in range(2):
                start = OFF - REACH + 2 * m + p
                cells = pad_ref[r, pl.ds(start, half, stride=2), :]
                pair_ref[m, pl.ds(pl.multiple_of(r * half, half), half), p * 128 : p * 128 + 128] = (
                    cells.astype(jnp.bfloat16)
                )
        return carry

    lax.fori_loop(0, pad_ref.shape[0], body, 0, unroll=2)


def fill_weights(kern_ref, w_ref, flip):
    width = kern_ref.shape[2]
    row = lax.broadcasted_iota(jnp.int32, (width, width), 0)
    col = lax.broadcasted_iota(jnp.int32, (width, width), 1)
    eye = row == col
    for a in range(TAPS):
        for m in range(PAIRS):
            for p in range(2):
                for q in range(2):
                    b = 2 * m + p - q
                    base = ((a * PAIRS + m) * 2 + p) * width
                    if 0 <= b < TAPS:
                        tap = (
                            kern_ref[TAPS - 1 - a, pl.ds(TAPS - 1 - b, 1), :]
                            if flip
                            else kern_ref[a, pl.ds(b, 1), :]
                        )
                        block = jnp.where(eye, jnp.broadcast_to(tap, (width, width)), 0.0)
                    else:
                        block = jnp.zeros((width, width), jnp.float32)
                    w_ref[base : base + width, q * width : (q + 1) * width] = block.astype(
                        jnp.bfloat16
                    )


def conv_pairs(pair_ref, w_ref, row0, row_count, half):
    lhs = jnp.concatenate(
        [
            pair_ref[m, pl.ds(pl.multiple_of((row0 + a) * half, half), row_count * half), :]
            for a in range(TAPS)
            for m in range(PAIRS)
        ],
        axis=1,
    )
    return jnp.dot(lhs, w_ref[...], preferred_element_type=jnp.float32)


def dot(left, right, dims):
    return lax.dot_general(left, right, (dims, ((), ())), preferred_element_type=jnp.float32)


def fold(values):
    return jnp.sum(values.reshape(-1, 8, values.shape[-1]), axis=0)


def tap_sums(pad_ref, cell_ref, row0, row_count, cols):
    sums = {}
    for b in range(TAPS):
        for a in range(TAPS):
            sums[a, b] = jnp.zeros((8, 128), jnp.float32)
        for s in range(0, cols, 8):
            grads = [cell_ref[r * cols + s : r * cols + s + 8, :] for r in range(row_count)]
            for reached in range(row_count + TAPS - 1):
                start = OFF - REACH + b + s
                cells = pad_ref[row0 + reached, start : start + 8, :]
                for a in range(TAPS):
                    if 0 <= reached - a < row_count:
                        sums[a, b] = sums[a, b] + cells * grads[reached - a]
    return sums


def layer_kernel(
    block_rows,
    own,
    top,
    bottom,
    left,
    right,
    cot_ref,
    kern_ref,
    kbias_ref,
    gain_ref,
    shift_ref,
    wup_ref,
    bup_ref,
    wdown_ref,
    scale_ref,
    dconv_ref,
    parts_ref,
    dwup_ref,
    dgt_ref,
    sums_ref,
    dbup_ref,
    dkern_ref,
    stage_ref,
    pad_ref,
    pair_ref,
    w_ref,
    cell_ref,
    conv_ref,
):
    step = pl.program_id(0)
    cols = own.shape[1]
    half = cols // 2
    count = block_rows * half

    @pl.when(step == 0)
    def _():
        fill_weights(kern_ref, w_ref, False)
        fill_padded(own, top, bottom, left, right, pad_ref)
        fill_pairs(pad_ref, pair_ref)
        dwup_ref[...] = jnp.zeros_like(dwup_ref)
        dgt_ref[...] = jnp.zeros_like(dgt_ref)
        sums_ref[...] = jnp.zeros_like(sums_ref)
        dbup_ref[...] = jnp.zeros_like(dbup_ref)
        dkern_ref[...] = jnp.zeros_like(dkern_ref)
        conv_ref[...] = conv_pairs(pair_ref, w_ref, 0, block_rows, half)

    conv = conv_ref[...]
    conv = jnp.concatenate([conv[:, :128], conv[:, 128:]], axis=0) + kbias_ref[...]
    gain = gain_ref[...]
    centred = conv - jnp.mean(conv, axis=-1, keepdims=True)
    inv_std = lax.rsqrt(jnp.mean(centred * centred, axis=-1, keepdims=True) + EPSILON)
    normed = centred * inv_std
    normal = (normed * gain + shift_ref[...]).astype(jnp.bfloat16)
    hidden = dot(normal, wup_ref[...], ((1,), (0,))) + bup_ref[...]
    cdf = 0.5 * (1.0 + lax.erf(hidden * 0.7071067811865476))
    active = (hidden * cdf).astype(jnp.bfloat16)
    slope = cdf + hidden * jnp.exp(-0.5 * hidden * hidden) * 0.3989422804014327
    cell_ref[...] = cot_ref[...].astype(jnp.float32)
    cot = jnp.concatenate([cell_ref[pl.ds(q, count, stride=2), :] for q in range(2)], axis=0)
    d_output = (cot * scale_ref[...]).astype(jnp.bfloat16)
    d_hidden = (dot(d_output, wdown_ref[...], ((1,), (1,))) * slope).astype(jnp.bfloat16)
    d_normal = dot(d_hidden, wup_ref[...], ((1,), (1,)))
    d_normed = d_normal * gain
    first = jnp.mean(d_normed, axis=-1, keepdims=True)
    second = jnp.mean(d_normed * normed, axis=-1, keepdims=True)
    d_conv = inv_std * (d_normed - first - normed * second)
    sums_ref[0] += fold(d_conv)
    sums_ref[1] += fold(d_normal * normed)
    sums_ref[2] += fold(d_normal)
    sums_ref[3] += fold(cot)
    dbup_ref[...] += fold(d_hidden.astype(jnp.float32))
    dwup_ref[...] += dot(normal, d_hidden, ((0,), (0,)))
    dgt_ref[...] += dot(cot.astype(jnp.bfloat16), active, ((0,), (0,)))
    for q in range(2):
        cell_ref[pl.ds(q, count, stride=2), :] = d_conv[q * count : (q + 1) * count]
    dconv_ref[...] = cell_ref[...].astype(jnp.bfloat16)
    following = jnp.minimum(step + 1, pl.num_programs(0) - 1)
    conv = conv_pairs(pair_ref, w_ref, following * block_rows, block_rows, half)
    taps = tap_sums(pad_ref, cell_ref, step * block_rows, block_rows, cols)
    conv_ref[...] = conv
    for (a, b), value in taps.items():
        dkern_ref[a, b] += value

    @pl.when(step == pl.num_programs(0) - 1)
    def _():
        stage_ref[...] = jnp.zeros_like(stage_ref)
        for k in range(LANES):
            lanes = slice(k * 128, k * 128 + 128)
            stage_ref[pl.ds(k, 128, stride=SHARE), :] = dwup_ref[:, lanes]
            stage_ref[pl.ds(LANES + k, 128, stride=SHARE), :] = dgt_ref[:, lanes]
        small = [dkern_ref[a, b] for a in range(TAPS) for b in range(TAPS)]
        small += [sums_ref[k] for k in range(4)]
        small += [dbup_ref[:, k * 128 : k * 128 + 128] for k in range(LANES)]
        for i, value in enumerate(small):
            at = i * SHARE + 2 * LANES
            stage_ref[at : at + 1, :] = jnp.sum(value, axis=0, keepdims=True)
        parts_ref[...] = stage_ref[...].astype(jnp.bfloat16)


def layer(x, sides, cotangent, kernel, kbias, gain, shift, wup, bup, wdown, scale):
    rows, cols, width = x.shape
    hidden = wup.shape[1]
    block_rows = 16
    block = block_rows * cols
    whole = lambda a: pl.BlockSpec(a.shape, lambda i: (0,) * a.ndim)
    row = lambda a: a.reshape(1, -1)
    consts = (kernel, row(kbias), row(gain), row(shift), wup, row(bup), wdown, row(scale))
    padded = rows + 2 * REACH
    cells = pl.BlockSpec((block, width), lambda i: (i, 0))
    full = lambda *shape: pl.BlockSpec(shape, lambda i: (0,) * len(shape))
    f32 = jnp.float32
    return pl.pallas_call(
        functools.partial(layer_kernel, block_rows),
        grid=(rows // block_rows,),
        in_specs=[whole(x)]
        + [whole(s) for s in sides]
        + [cells]
        + [whole(c) for c in consts],
        out_specs=[cells, full(width * SHARE, width)],
        out_shape=[
            jax.ShapeDtypeStruct((rows * cols, width), jnp.bfloat16),
            jax.ShapeDtypeStruct((width * SHARE, width), jnp.bfloat16),
        ],
        scratch_shapes=[
            pltpu.VMEM((width, hidden), f32),
            pltpu.VMEM((width, hidden), f32),
            pltpu.VMEM((4, 8, width), f32),
            pltpu.VMEM((8, hidden), f32),
            pltpu.VMEM((TAPS, TAPS, 8, width), f32),
            pltpu.VMEM((width * SHARE, width), f32),
            pltpu.VMEM((padded, cols + 2 * OFF, width), f32),
            pltpu.VMEM((PAIRS, padded * cols // 2, 2 * width), jnp.bfloat16),
            pltpu.VMEM((TAPS * PAIRS * 2 * width, 2 * width), jnp.bfloat16),
            pltpu.VMEM((block, width), f32),
            pltpu.VMEM((block // 2, 2 * width), f32),
        ],
        compiler_params=pltpu.CompilerParams(vmem_limit_bytes=GRANT),
        name="layer",
    )(x, *sides, cotangent.reshape(rows * cols, width), *consts)


def spread_kernel(
    block_rows, own, top, bottom, left, right, cot_ref, kern_ref, out_ref, pad_ref, pair_ref, w_ref, cell_ref
):
    step = pl.program_id(0)
    half = own.shape[1] // 2
    count = block_rows * half

    @pl.when(step == 0)
    def _():
        fill_weights(kern_ref, w_ref, True)
        fill_padded(own, top, bottom, left, right, pad_ref)
        fill_pairs(pad_ref, pair_ref)

    conv = conv_pairs(pair_ref, w_ref, step * block_rows, block_rows, half)
    for q in range(2):
        cell_ref[pl.ds(q, count, stride=2), :] = conv[:, q * 128 : q * 128 + 128]
    out_ref[...] = (cell_ref[...] + cot_ref[...].astype(jnp.float32)).astype(jnp.bfloat16)


def spread(dconv, sides, cotangent, kernel):
    rows, cols, width = dconv.shape
    block_rows = 16
    block = block_rows * cols
    padded = rows + 2 * REACH
    whole = lambda a: pl.BlockSpec(a.shape, lambda i: (0,) * a.ndim)
    cells = pl.BlockSpec((block, width), lambda i: (i, 0))
    return pl.pallas_call(
        functools.partial(spread_kernel, block_rows),
        grid=(rows // block_rows,),
        in_specs=[whole(dconv)] + [whole(s) for s in sides] + [cells, whole(kernel)],
        out_specs=cells,
        out_shape=jax.ShapeDtypeStruct((rows * cols, width), jnp.bfloat16),
        scratch_shapes=[
            pltpu.VMEM((padded, cols + 2 * OFF, width), jnp.float32),
            pltpu.VMEM((PAIRS, padded * cols // 2, 2 * width), jnp.bfloat16),
            pltpu.VMEM((TAPS * PAIRS * 2 * width, 2 * width), jnp.bfloat16),
            pltpu.VMEM((block, width), jnp.float32),
        ],
        compiler_params=pltpu.CompilerParams(vmem_limit_bytes=GRANT),
        name="spread",
    )(dconv, *sides, cotangent.reshape(rows * cols, width), kernel).reshape(rows, cols, width)


def total(parts):
    axes = ("gx", "gy")
    share = lax.all_to_all(parts, axes, split_axis=0, concat_axis=0, tiled=True)
    share = jnp.sum(share.astype(jnp.float32), axis=0).astype(parts.dtype)
    copies = jnp.broadcast_to(share[None], parts.shape)
    return lax.all_to_all(copies, axes, split_axis=0, concat_axis=0, tiled=True)


def finish_kernel(
    factor,
    summed_ref,
    wdown_ref,
    bdown_ref,
    scale_ref,
    dkern_ref,
    dkbias_ref,
    dgain_ref,
    dshift_ref,
    dwup_ref,
    dbup_ref,
    dwdown_ref,
    dbdown_ref,
    dscale_ref,
    stage_ref,
):
    stage_ref[...] = summed_ref[...].astype(jnp.float32) * factor
    scale = scale_ref[...]

    def small(i):
        at = i * SHARE + 2 * LANES
        return stage_ref[at : at + 1, :]

    for a in range(TAPS):
        for b in range(TAPS):
            dkern_ref[a, b : b + 1, :] = small(a * TAPS + b)
    first = TAPS * TAPS
    dkbias_ref[...] = small(first)
    dgain_ref[...] = small(first + 1)
    dshift_ref[...] = small(first + 2)
    cot_sum = small(first + 3)
    dscale = bdown_ref[...] * cot_sum
    for k in range(LANES):
        lanes = slice(k * 128, k * 128 + 128)
        dbup_ref[:, lanes] = small(first + 4 + k)
        dwup_ref[:, lanes] = stage_ref[pl.ds(k, 128, stride=SHARE), :]
        product = stage_ref[pl.ds(LANES + k, 128, stride=SHARE), :].T
        dwdown_ref[lanes, :] = product * scale
        weights = wdown_ref[lanes, :].astype(jnp.float32)
        dscale = dscale + jnp.sum(product * weights, axis=0, keepdims=True)
    dbdown_ref[...] = cot_sum * scale
    dscale_ref[...] = dscale


def finish(summed, w_down, b_down, layer_scale, factor):
    hidden, width = w_down.shape
    shapes = [(TAPS, TAPS, width)] + [(1, width)] * 3 + [(width, hidden), (1, hidden), (hidden, width)]
    shapes += [(1, width)] * 2
    row = lambda a: a.reshape(1, -1)
    return pl.pallas_call(
        functools.partial(finish_kernel, factor),
        out_shape=[jax.ShapeDtypeStruct(shape, jnp.float32) for shape in shapes],
        scratch_shapes=[pltpu.VMEM(summed.shape, jnp.float32)],
        name="finish",
    )(summed, w_down, row(b_down), row(layer_scale))


def local(
    features, cotangent, kernel, kernel_bias, norm_gain, norm_shift, w_up, b_up, w_down, b_down, layer_scale
):
    rows, cols, width = features.shape
    devices = lax.axis_size("gx") * lax.axis_size("gy")
    dconv, parts = layer(
        features,
        halo(features),
        cotangent,
        kernel,
        kernel_bias,
        norm_gain,
        norm_shift,
        w_up,
        b_up,
        w_down,
        layer_scale,
    )
    dconv = dconv.reshape(rows, cols, width)
    d_features = spread(dconv, halo(dconv), cotangent, kernel)
    summed = total(parts.reshape(devices, SHARE, width)).reshape(devices * SHARE, width)
    factor = 1.0 / math.sqrt(rows * cols * devices)
    grads = finish(summed, w_down, b_down, layer_scale, factor)
    return (d_features,) + tuple(g.reshape(-1) if g.shape[0] == 1 else g for g in grads)


def solution(mesh):
    placed = (P("gx", "gy", None), P("gx", "gy", None), P(), P(), P(), P(), P(), P(), P(), P(), P())
    return jax.shard_map(
        local,
        mesh=mesh,
        in_specs=placed,
        out_specs=(P("gx", "gy", None), P(), P(), P(), P(), P(), P(), P(), P(), P()),
        check_vma=False,
    )
```

```python
import functools
import math

import jax
import jax.numpy as jnp
from jax import lax
from jax.experimental import pallas as pl
from jax.experimental.pallas import tpu as pltpu
from jax.sharding import PartitionSpec as P

EPSILON = 1e-06
REACH = 3
TAPS = 7
PAIRS = 4
OFF = 8
GRANT = 58 * 2**20
LANES = 4
SHARE = 16


def shifted(cells, axis, step, cyclic):
    count = lax.axis_size(axis)
    pairs = [(i, (i + step) % count) for i in range(count) if cyclic or 0 <= i + step < count]
    return lax.ppermute(cells, axis, pairs)


def halo(cells):
    rows, cols = cells.shape[0], cells.shape[1]
    top = shifted(cells[rows - REACH :], "gx", 1, True)
    bottom = shifted(cells[:REACH], "gx", -1, True)

    def edge(start):
        cut = [part[:, start : start + REACH] for part in (top, cells, bottom)]
        return jnp.concatenate(cut, axis=0)

    left = shifted(edge(cols - REACH), "gy", 1, False)
    right = shifted(edge(0), "gy", -1, False)
    return top, bottom, left, right


def fill_padded(own, top, bottom, left, right, pad_ref):
    rows, cols = own.shape[0], own.shape[1]
    inner = pl.ds(OFF, cols)
    pad_ref[0:REACH, inner, :] = top[...].astype(jnp.float32)
    pad_ref[REACH + rows : 2 * REACH + rows, inner, :] = bottom[...].astype(jnp.float32)

    def body(r, carry):
        pad_ref[REACH + r, inner, :] = own[r].astype(jnp.float32)
        return carry

    lax.fori_loop(0, rows, body, 0, unroll=4)

    def sides(r, carry):
        pad_ref[r, OFF - REACH : OFF, :] = left[r].astype(jnp.float32)
        pad_ref[r, OFF + cols : OFF + cols + REACH, :] = right[r].astype(jnp.float32)
        return carry

    lax.fori_loop(0, rows + 2 * REACH, sides, 0, unroll=2)


def fill_pairs(pad_ref, pair_ref):
    half = pair_ref.shape[1] // pad_ref.shape[0]

    def body(r, carry):
        for m in range(PAIRS):
            for p in range(2):
                start = OFF - REACH + 2 * m + p
                cells = pad_ref[r, pl.ds(start, half, stride=2), :]
                pair_ref[m, pl.ds(pl.multiple_of(r * half, half), half), p * 128 : p * 128 + 128] = (
                    cells.astype(jnp.bfloat16)
                )
        return carry

    lax.fori_loop(0, pad_ref.shape[0], body, 0, unroll=2)


def fill_weights(kern_ref, w_ref, flip):
    width = kern_ref.shape[2]
    row = lax.broadcasted_iota(jnp.int32, (width, width), 0)
    col = lax.broadcasted_iota(jnp.int32, (width, width), 1)
    eye = row == col
    for a in range(TAPS):
        for m in range(PAIRS):
            for p in range(2):
                for q in range(2):
                    b = 2 * m + p - q
                    base = ((a * PAIRS + m) * 2 + p) * width
                    if 0 <= b < TAPS:
                        tap = (
                            kern_ref[TAPS - 1 - a, pl.ds(TAPS - 1 - b, 1), :]
                            if flip
                            else kern_ref[a, pl.ds(b, 1), :]
                        )
                        block = jnp.where(eye, jnp.broadcast_to(tap, (width, width)), 0.0)
                    else:
                        block = jnp.zeros((width, width), jnp.float32)
                    w_ref[base : base + width, q * width : (q + 1) * width] = block.astype(
                        jnp.bfloat16
                    )


def conv_pairs(pair_ref, w_ref, row0, row_count, half):
    lhs = jnp.concatenate(
        [
            pair_ref[m, pl.ds(pl.multiple_of((row0 + a) * half, half), row_count * half), :]
            for a in range(TAPS)
            for m in range(PAIRS)
        ],
        axis=1,
    )
    return jnp.dot(lhs, w_ref[...], preferred_element_type=jnp.float32)


def dot(left, right, dims):
    return lax.dot_general(left, right, (dims, ((), ())), preferred_element_type=jnp.float32)


def fold(values):
    return jnp.sum(values.reshape(-1, 8, values.shape[-1]), axis=0)


def tap_sums(pad_ref, cell_ref, row0, row_count, cols):
    sums = {}
    for b in range(TAPS):
        for a in range(TAPS):
            sums[a, b] = jnp.zeros((8, 128), jnp.float32)
        for s in range(0, cols, 8):
            grads = [cell_ref[r * cols + s : r * cols + s + 8, :] for r in range(row_count)]
            for reached in range(row_count + TAPS - 1):
                start = OFF - REACH + b + s
                cells = pad_ref[row0 + reached, start : start + 8, :]
                for a in range(TAPS):
                    if 0 <= reached - a < row_count:
                        sums[a, b] = sums[a, b] + cells * grads[reached - a]
    return sums


def layer_kernel(
    block_rows,
    own,
    top,
    bottom,
    left,
    right,
    cot_ref,
    kern_ref,
    kbias_ref,
    gain_ref,
    shift_ref,
    wup_ref,
    bup_ref,
    wdown_ref,
    scale_ref,
    dconv_ref,
    dwup_ref,
    dgt_ref,
    sums_ref,
    dbup_ref,
    dkern_ref,
    pad_ref,
    pair_ref,
    w_ref,
    cell_ref,
    conv_ref,
):
    step = pl.program_id(0)
    cols = own.shape[1]
    half = cols // 2
    count = block_rows * half

    @pl.when(step == 0)
    def _():
        fill_weights(kern_ref, w_ref, False)
        fill_padded(own, top, bottom, left, right, pad_ref)
        fill_pairs(pad_ref, pair_ref)
        dwup_ref[...] = jnp.zeros_like(dwup_ref)
        dgt_ref[...] = jnp.zeros_like(dgt_ref)
        sums_ref[...] = jnp.zeros_like(sums_ref)
        dbup_ref[...] = jnp.zeros_like(dbup_ref)
        dkern_ref[...] = jnp.zeros_like(dkern_ref)
        conv_ref[...] = conv_pairs(pair_ref, w_ref, 0, block_rows, half)

    conv = conv_ref[...]
    conv = jnp.concatenate([conv[:, :128], conv[:, 128:]], axis=0) + kbias_ref[...]
    gain = gain_ref[...]
    centred = conv - jnp.mean(conv, axis=-1, keepdims=True)
    inv_std = lax.rsqrt(jnp.mean(centred * centred, axis=-1, keepdims=True) + EPSILON)
    normed = centred * inv_std
    normal = (normed * gain + shift_ref[...]).astype(jnp.bfloat16)
    hidden = dot(normal, wup_ref[...], ((1,), (0,))) + bup_ref[...]
    cdf = 0.5 * (1.0 + lax.erf(hidden * 0.7071067811865476))
    active = (hidden * cdf).astype(jnp.bfloat16)
    slope = cdf + hidden * jnp.exp(-0.5 * hidden * hidden) * 0.3989422804014327
    cell_ref[...] = cot_ref[...].astype(jnp.float32)
    cot = jnp.concatenate([cell_ref[pl.ds(q, count, stride=2), :] for q in range(2)], axis=0)
    d_output = (cot * scale_ref[...]).astype(jnp.bfloat16)
    d_hidden = (dot(d_output, wdown_ref[...], ((1,), (1,))) * slope).astype(jnp.bfloat16)
    d_normal = dot(d_hidden, wup_ref[...], ((1,), (1,)))
    d_normed = d_normal * gain
    first = jnp.mean(d_normed, axis=-1, keepdims=True)
    second = jnp.mean(d_normed * normed, axis=-1, keepdims=True)
    d_conv = inv_std * (d_normed - first - normed * second)
    sums_ref[0] += fold(d_conv)
    sums_ref[1] += fold(d_normal * normed)
    sums_ref[2] += fold(d_normal)
    sums_ref[3] += fold(cot)
    dbup_ref[...] += fold(d_hidden.astype(jnp.float32))
    dwup_ref[...] += dot(normal, d_hidden, ((0,), (0,)))
    dgt_ref[...] += dot(cot.astype(jnp.bfloat16), active, ((0,), (0,)))
    for q in range(2):
        cell_ref[pl.ds(q, count, stride=2), :] = d_conv[q * count : (q + 1) * count]
    dconv_ref[...] = cell_ref[...].astype(jnp.bfloat16)
    following = jnp.minimum(step + 1, pl.num_programs(0) - 1)
    conv = conv_pairs(pair_ref, w_ref, following * block_rows, block_rows, half)
    taps = tap_sums(pad_ref, cell_ref, step * block_rows, block_rows, cols)
    conv_ref[...] = conv
    for (a, b), value in taps.items():
        dkern_ref[a, b] += value


def layer(x, sides, cotangent, kernel, kbias, gain, shift, wup, bup, wdown, scale):
    rows, cols, width = x.shape
    hidden = wup.shape[1]
    block_rows = 16
    block = block_rows * cols
    whole = lambda a: pl.BlockSpec(a.shape, lambda i: (0,) * a.ndim)
    row = lambda a: a.reshape(1, -1)
    consts = (kernel, row(kbias), row(gain), row(shift), wup, row(bup), wdown, row(scale))
    padded = rows + 2 * REACH
    cells = pl.BlockSpec((block, width), lambda i: (i, 0))
    full = lambda *shape: pl.BlockSpec(shape, lambda i: (0,) * len(shape))
    f32 = jnp.float32
    return pl.pallas_call(
        functools.partial(layer_kernel, block_rows),
        grid=(rows // block_rows,),
        in_specs=[whole(x)]
        + [whole(s) for s in sides]
        + [cells]
        + [whole(c) for c in consts],
        out_specs=[
            cells,
            full(width, hidden),
            full(width, hidden),
            full(4, 8, width),
            full(8, hidden),
            full(TAPS, TAPS, 8, width),
        ],
        out_shape=[
            jax.ShapeDtypeStruct((rows * cols, width), jnp.bfloat16),
            jax.ShapeDtypeStruct((width, hidden), f32),
            jax.ShapeDtypeStruct((width, hidden), f32),
            jax.ShapeDtypeStruct((4, 8, width), f32),
            jax.ShapeDtypeStruct((8, hidden), f32),
            jax.ShapeDtypeStruct((TAPS, TAPS, 8, width), f32),
        ],
        scratch_shapes=[
            pltpu.VMEM((padded, cols + 2 * OFF, width), f32),
            pltpu.VMEM((PAIRS, padded * cols // 2, 2 * width), jnp.bfloat16),
            pltpu.VMEM((TAPS * PAIRS * 2 * width, 2 * width), jnp.bfloat16),
            pltpu.VMEM((block, width), f32),
            pltpu.VMEM((block // 2, 2 * width), f32),
        ],
        compiler_params=pltpu.CompilerParams(vmem_limit_bytes=GRANT),
        name="layer",
    )(x, *sides, cotangent.reshape(rows * cols, width), *consts)


def parts_kernel(dwup_ref, dgt_ref, sums_ref, dbup_ref, dkern_ref, parts_ref, stage_ref):
    stage_ref[...] = jnp.zeros_like(stage_ref)
    for k in range(LANES):
        lanes = slice(k * 128, k * 128 + 128)
        stage_ref[pl.ds(k, 128, stride=SHARE), :] = dwup_ref[:, lanes]
        stage_ref[pl.ds(LANES + k, 128, stride=SHARE), :] = dgt_ref[:, lanes]
    small = [dkern_ref[a, b] for a in range(TAPS) for b in range(TAPS)]
    small += [sums_ref[k] for k in range(4)]
    small += [dbup_ref[:, k * 128 : k * 128 + 128] for k in range(LANES)]
    for i, value in enumerate(small):
        at = i * SHARE + 2 * LANES
        stage_ref[at : at + 1, :] = jnp.sum(value, axis=0, keepdims=True)
    parts_ref[...] = stage_ref[...].astype(jnp.bfloat16)


def shares(*sums):
    width = sums[0].shape[0]
    return pl.pallas_call(
        parts_kernel,
        out_shape=jax.ShapeDtypeStruct((width * SHARE, width), jnp.bfloat16),
        scratch_shapes=[pltpu.VMEM((width * SHARE, width), jnp.float32)],
        name="shares",
    )(*sums)


def spread_kernel(
    block_rows, own, top, bottom, left, right, cot_ref, kern_ref, out_ref, pad_ref, pair_ref, w_ref, cell_ref
):
    step = pl.program_id(0)
    half = own.shape[1] // 2
    count = block_rows * half

    @pl.when(step == 0)
    def _():
        fill_weights(kern_ref, w_ref, True)
        fill_padded(own, top, bottom, left, right, pad_ref)
        fill_pairs(pad_ref, pair_ref)

    conv = conv_pairs(pair_ref, w_ref, step * block_rows, block_rows, half)
    for q in range(2):
        cell_ref[pl.ds(q, count, stride=2), :] = conv[:, q * 128 : q * 128 + 128]
    out_ref[...] = (cell_ref[...] + cot_ref[...].astype(jnp.float32)).astype(jnp.bfloat16)


def spread(dconv, sides, cotangent, kernel):
    rows, cols, width = dconv.shape
    block_rows = 16
    block = block_rows * cols
    padded = rows + 2 * REACH
    whole = lambda a: pl.BlockSpec(a.shape, lambda i: (0,) * a.ndim)
    cells = pl.BlockSpec((block, width), lambda i: (i, 0))
    return pl.pallas_call(
        functools.partial(spread_kernel, block_rows),
        grid=(rows // block_rows,),
        in_specs=[whole(dconv)] + [whole(s) for s in sides] + [cells, whole(kernel)],
        out_specs=cells,
        out_shape=jax.ShapeDtypeStruct((rows * cols, width), jnp.bfloat16),
        scratch_shapes=[
            pltpu.VMEM((padded, cols + 2 * OFF, width), jnp.float32),
            pltpu.VMEM((PAIRS, padded * cols // 2, 2 * width), jnp.bfloat16),
            pltpu.VMEM((TAPS * PAIRS * 2 * width, 2 * width), jnp.bfloat16),
            pltpu.VMEM((block, width), jnp.float32),
        ],
        compiler_params=pltpu.CompilerParams(vmem_limit_bytes=GRANT),
        name="spread",
    )(dconv, *sides, cotangent.reshape(rows * cols, width), kernel).reshape(rows, cols, width)


def total(parts):
    axes = ("gx", "gy")
    share = lax.all_to_all(parts, axes, split_axis=0, concat_axis=0, tiled=True)
    share = jnp.sum(share.astype(jnp.float32), axis=0).astype(parts.dtype)
    copies = jnp.broadcast_to(share[None], parts.shape)
    return lax.all_to_all(copies, axes, split_axis=0, concat_axis=0, tiled=True)


def finish_kernel(
    factor,
    summed_ref,
    wdown_ref,
    bdown_ref,
    scale_ref,
    dkern_ref,
    dkbias_ref,
    dgain_ref,
    dshift_ref,
    dwup_ref,
    dbup_ref,
    dwdown_ref,
    dbdown_ref,
    dscale_ref,
    stage_ref,
):
    stage_ref[...] = summed_ref[...].astype(jnp.float32) * factor
    scale = scale_ref[...]

    def small(i):
        at = i * SHARE + 2 * LANES
        return stage_ref[at : at + 1, :]

    for a in range(TAPS):
        for b in range(TAPS):
            dkern_ref[a, b : b + 1, :] = small(a * TAPS + b)
    first = TAPS * TAPS
    dkbias_ref[...] = small(first)
    dgain_ref[...] = small(first + 1)
    dshift_ref[...] = small(first + 2)
    cot_sum = small(first + 3)
    dscale = bdown_ref[...] * cot_sum
    for k in range(LANES):
        lanes = slice(k * 128, k * 128 + 128)
        dbup_ref[:, lanes] = small(first + 4 + k)
        dwup_ref[:, lanes] = stage_ref[pl.ds(k, 128, stride=SHARE), :]
        product = stage_ref[pl.ds(LANES + k, 128, stride=SHARE), :].T
        dwdown_ref[lanes, :] = product * scale
        weights = wdown_ref[lanes, :].astype(jnp.float32)
        dscale = dscale + jnp.sum(product * weights, axis=0, keepdims=True)
    dbdown_ref[...] = cot_sum * scale
    dscale_ref[...] = dscale


def finish(summed, w_down, b_down, layer_scale, factor):
    hidden, width = w_down.shape
    shapes = [(TAPS, TAPS, width)] + [(1, width)] * 3 + [(width, hidden), (1, hidden), (hidden, width)]
    shapes += [(1, width)] * 2
    row = lambda a: a.reshape(1, -1)
    return pl.pallas_call(
        functools.partial(finish_kernel, factor),
        out_shape=[jax.ShapeDtypeStruct(shape, jnp.float32) for shape in shapes],
        scratch_shapes=[pltpu.VMEM(summed.shape, jnp.float32)],
        name="finish",
    )(summed, w_down, row(b_down), row(layer_scale))


def local(
    features, cotangent, kernel, kernel_bias, norm_gain, norm_shift, w_up, b_up, w_down, b_down, layer_scale
):
    rows, cols, width = features.shape
    devices = lax.axis_size("gx") * lax.axis_size("gy")
    dconv, *sums = layer(
        features,
        halo(features),
        cotangent,
        kernel,
        kernel_bias,
        norm_gain,
        norm_shift,
        w_up,
        b_up,
        w_down,
        layer_scale,
    )
    dconv = dconv.reshape(rows, cols, width)
    d_features = spread(dconv, halo(dconv), cotangent, kernel)
    summed = total(shares(*sums).reshape(devices, SHARE, width)).reshape(devices * SHARE, width)
    factor = 1.0 / math.sqrt(rows * cols * devices)
    grads = finish(summed, w_down, b_down, layer_scale, factor)
    return (d_features,) + tuple(g.reshape(-1) if g.shape[0] == 1 else g for g in grads)


def solution(mesh):
    placed = (P("gx", "gy", None), P("gx", "gy", None), P(), P(), P(), P(), P(), P(), P(), P(), P())
    return jax.shard_map(
        local,
        mesh=mesh,
        in_specs=placed,
        out_specs=(P("gx", "gy", None), P(), P(), P(), P(), P(), P(), P(), P(), P()),
        check_vma=False,
    )
```

```python
import functools
import math

import jax
import jax.numpy as jnp
from jax import lax
from jax.experimental import pallas as pl
from jax.experimental.pallas import tpu as pltpu
from jax.sharding import PartitionSpec as P

EPSILON = 1e-06
REACH = 3
TAPS = 7
PAIRS = 4
OFF = 8
GRANT = 58 * 2**20
VECTOR_ROWS = 8
LANES = 4
SHARE = 16


def shifted(cells, axis, step, cyclic):
    count = lax.axis_size(axis)
    pairs = [(i, (i + step) % count) for i in range(count) if cyclic or 0 <= i + step < count]
    return lax.ppermute(cells, axis, pairs)


def halo(cells):
    rows, cols = cells.shape[0], cells.shape[1]
    top = shifted(cells[rows - REACH :], "gx", 1, True)
    bottom = shifted(cells[:REACH], "gx", -1, True)

    def edge(start):
        cut = [part[:, start : start + REACH] for part in (top, cells, bottom)]
        return jnp.concatenate(cut, axis=0)

    left = shifted(edge(cols - REACH), "gy", 1, False)
    right = shifted(edge(0), "gy", -1, False)
    return top, bottom, left, right


def fill_padded(own, top, bottom, left, right, pad_ref):
    rows, cols = own.shape[0], own.shape[1]
    inner = pl.ds(OFF, cols)
    pad_ref[0:REACH, inner, :] = top[...].astype(jnp.float32)
    pad_ref[REACH + rows : 2 * REACH + rows, inner, :] = bottom[...].astype(jnp.float32)

    def body(r, carry):
        pad_ref[REACH + r, inner, :] = own[r].astype(jnp.float32)
        return carry

    lax.fori_loop(0, rows, body, 0, unroll=4)

    def sides(r, carry):
        pad_ref[r, OFF - REACH : OFF, :] = left[r].astype(jnp.float32)
        pad_ref[r, OFF + cols : OFF + cols + REACH, :] = right[r].astype(jnp.float32)
        return carry

    lax.fori_loop(0, rows + 2 * REACH, sides, 0, unroll=2)


def fill_pairs(pad_ref, pair_ref):
    half = pair_ref.shape[1] // pad_ref.shape[0]

    def body(r, carry):
        for m in range(PAIRS):
            for p in range(2):
                start = OFF - REACH + 2 * m + p
                cells = pad_ref[r, pl.ds(start, half, stride=2), :]
                pair_ref[m, pl.ds(pl.multiple_of(r * half, half), half), p * 128 : p * 128 + 128] = (
                    cells.astype(jnp.bfloat16)
                )
        return carry

    lax.fori_loop(0, pad_ref.shape[0], body, 0, unroll=2)


def fill_weights(kern_ref, w_ref, flip):
    width = kern_ref.shape[2]
    row = lax.broadcasted_iota(jnp.int32, (width, width), 0)
    col = lax.broadcasted_iota(jnp.int32, (width, width), 1)
    eye = row == col
    for a in range(TAPS):
        for m in range(PAIRS):
            for p in range(2):
                for q in range(2):
                    b = 2 * m + p - q
                    base = ((a * PAIRS + m) * 2 + p) * width
                    if 0 <= b < TAPS:
                        tap = (
                            kern_ref[TAPS - 1 - a, pl.ds(TAPS - 1 - b, 1), :]
                            if flip
                            else kern_ref[a, pl.ds(b, 1), :]
                        )
                        block = jnp.where(eye, jnp.broadcast_to(tap, (width, width)), 0.0)
                    else:
                        block = jnp.zeros((width, width), jnp.float32)
                    w_ref[base : base + width, q * width : (q + 1) * width] = block.astype(
                        jnp.bfloat16
                    )


def conv_pairs(pair_ref, w_ref, row0, row_count, half):
    lhs = jnp.concatenate(
        [
            pair_ref[m, pl.ds(pl.multiple_of((row0 + a) * half, half), row_count * half), :]
            for a in range(TAPS)
            for m in range(PAIRS)
        ],
        axis=1,
    )
    return jnp.dot(lhs, w_ref[...], preferred_element_type=jnp.float32)


def dot(left, right, dims):
    return lax.dot_general(left, right, (dims, ((), ())), preferred_element_type=jnp.float32)


def fold(values):
    return jnp.sum(values.reshape(-1, 8, values.shape[-1]), axis=0)


def tap_sums(pad_ref, cell_ref, row0, row_count, cols):
    sums = {}
    for b in range(TAPS):
        for a in range(TAPS):
            sums[a, b] = jnp.zeros((8, 128), jnp.float32)
        for s in range(0, cols, 8):
            grads = [cell_ref[r * cols + s : r * cols + s + 8, :] for r in range(row_count)]
            for reached in range(row_count + TAPS - 1):
                start = OFF - REACH + b + s
                cells = pad_ref[row0 + reached, start : start + 8, :]
                for a in range(TAPS):
                    if 0 <= reached - a < row_count:
                        sums[a, b] = sums[a, b] + cells * grads[reached - a]
    return sums


def layer_kernel(
    block_rows,
    own,
    top,
    bottom,
    left,
    right,
    cot_ref,
    kern_ref,
    kbias_ref,
    gain_ref,
    shift_ref,
    wup_ref,
    bup_ref,
    wdown_ref,
    scale_ref,
    dconv_ref,
    dwup_ref,
    dgt_ref,
    sums_ref,
    dbup_ref,
    dkern_ref,
    pad_ref,
    pair_ref,
    w_ref,
    cell_ref,
    conv_ref,
):
    step = pl.program_id(0)
    cols = own.shape[1]
    half = cols // 2
    count = block_rows * half

    @pl.when(step == 0)
    def _():
        fill_weights(kern_ref, w_ref, False)
        fill_padded(own, top, bottom, left, right, pad_ref)
        fill_pairs(pad_ref, pair_ref)
        dwup_ref[...] = jnp.zeros_like(dwup_ref)
        dgt_ref[...] = jnp.zeros_like(dgt_ref)
        sums_ref[...] = jnp.zeros_like(sums_ref)
        dbup_ref[...] = jnp.zeros_like(dbup_ref)
        dkern_ref[...] = jnp.zeros_like(dkern_ref)
        conv_ref[...] = conv_pairs(pair_ref, w_ref, 0, block_rows, half)

    conv = conv_ref[...]
    conv = jnp.concatenate([conv[:, :128], conv[:, 128:]], axis=0) + kbias_ref[...]
    gain = gain_ref[...]
    centred = conv - jnp.mean(conv, axis=-1, keepdims=True)
    inv_std = lax.rsqrt(jnp.mean(centred * centred, axis=-1, keepdims=True) + EPSILON)
    normed = centred * inv_std
    normal = (normed * gain + shift_ref[...]).astype(jnp.bfloat16)
    hidden = dot(normal, wup_ref[...], ((1,), (0,))) + bup_ref[...]
    cdf = 0.5 * (1.0 + lax.erf(hidden * 0.7071067811865476))
    active = (hidden * cdf).astype(jnp.bfloat16)
    slope = cdf + hidden * jnp.exp(-0.5 * hidden * hidden) * 0.3989422804014327
    cell_ref[...] = cot_ref[...].astype(jnp.float32)
    cot = jnp.concatenate([cell_ref[pl.ds(q, count, stride=2), :] for q in range(2)], axis=0)
    d_output = (cot * scale_ref[...]).astype(jnp.bfloat16)
    d_hidden = (dot(d_output, wdown_ref[...], ((1,), (1,))) * slope).astype(jnp.bfloat16)
    d_normal = dot(d_hidden, wup_ref[...], ((1,), (1,)))
    d_normed = d_normal * gain
    first = jnp.mean(d_normed, axis=-1, keepdims=True)
    second = jnp.mean(d_normed * normed, axis=-1, keepdims=True)
    d_conv = inv_std * (d_normed - first - normed * second)
    sums_ref[0] += fold(d_conv)
    sums_ref[1] += fold(d_normal * normed)
    sums_ref[2] += fold(d_normal)
    sums_ref[3] += fold(cot)
    dbup_ref[...] += fold(d_hidden.astype(jnp.float32))
    dwup_ref[...] += dot(normal, d_hidden, ((0,), (0,)))
    dgt_ref[...] += dot(cot.astype(jnp.bfloat16), active, ((0,), (0,)))
    for q in range(2):
        cell_ref[pl.ds(q, count, stride=2), :] = d_conv[q * count : (q + 1) * count]
    dconv_ref[...] = cell_ref[...].astype(jnp.bfloat16)
    @pl.when(step < pl.num_programs(0))
    def _():
        following = jnp.minimum(step + 1, pl.num_programs(0) - 1)
        taps = tap_sums(pad_ref, cell_ref, step * block_rows, block_rows, cols)
        conv = conv_pairs(pair_ref, w_ref, following * block_rows, block_rows, half)
        conv_ref[...] = conv
        for (a, b), value in taps.items():
            dkern_ref[a, b] += value


def layer(x, sides, cotangent, kernel, kbias, gain, shift, wup, bup, wdown, scale):
    rows, cols, width = x.shape
    hidden = wup.shape[1]
    block_rows = 16
    block = block_rows * cols
    whole = lambda a: pl.BlockSpec(a.shape, lambda i: (0,) * a.ndim)
    row = lambda a: a.reshape(1, -1)
    consts = (kernel, row(kbias), row(gain), row(shift), wup, row(bup), wdown, row(scale))
    padded = rows + 2 * REACH
    cells = pl.BlockSpec((block, width), lambda i: (i, 0))
    full = lambda *shape: pl.BlockSpec(shape, lambda i: (0,) * len(shape))
    f32 = jnp.float32
    return pl.pallas_call(
        functools.partial(layer_kernel, block_rows),
        grid=(rows // block_rows,),
        in_specs=[whole(x)]
        + [whole(s) for s in sides]
        + [cells]
        + [whole(c) for c in consts],
        out_specs=[
            cells,
            full(width, hidden),
            full(width, hidden),
            full(4, 8, width),
            full(8, hidden),
            full(TAPS, TAPS, 8, width),
        ],
        out_shape=[
            jax.ShapeDtypeStruct((rows * cols, width), jnp.bfloat16),
            jax.ShapeDtypeStruct((width, hidden), f32),
            jax.ShapeDtypeStruct((width, hidden), f32),
            jax.ShapeDtypeStruct((4, 8, width), f32),
            jax.ShapeDtypeStruct((8, hidden), f32),
            jax.ShapeDtypeStruct((TAPS, TAPS, 8, width), f32),
        ],
        scratch_shapes=[
            pltpu.VMEM((padded, cols + 2 * OFF, width), f32),
            pltpu.VMEM((PAIRS, padded * cols // 2, 2 * width), jnp.bfloat16),
            pltpu.VMEM((TAPS * PAIRS * 2 * width, 2 * width), jnp.bfloat16),
            pltpu.VMEM((block, width), f32),
            pltpu.VMEM((block // 2, 2 * width), f32),
        ],
        compiler_params=pltpu.CompilerParams(vmem_limit_bytes=GRANT),
        name="layer",
    )(x, *sides, cotangent.reshape(rows * cols, width), *consts)


def parts_kernel(dwup_ref, dgt_ref, sums_ref, dbup_ref, dkern_ref, parts_ref, stage_ref):
    stage_ref[...] = jnp.zeros_like(stage_ref)
    for k in range(LANES):
        lanes = slice(k * 128, k * 128 + 128)
        stage_ref[pl.ds(k, 128, stride=SHARE), :] = dwup_ref[:, lanes]
        stage_ref[pl.ds(LANES + k, 128, stride=SHARE), :] = dgt_ref[:, lanes]
    small = [dkern_ref[a, b] for a in range(TAPS) for b in range(TAPS)]
    small += [sums_ref[k] for k in range(4)]
    small += [dbup_ref[:, k * 128 : k * 128 + 128] for k in range(LANES)]
    for i, value in enumerate(small):
        at = i * SHARE + 2 * LANES
        stage_ref[at : at + 1, :] = jnp.sum(value, axis=0, keepdims=True)
    parts_ref[...] = stage_ref[...].astype(jnp.bfloat16)


def shares(*sums):
    width = sums[0].shape[0]
    return pl.pallas_call(
        parts_kernel,
        out_shape=jax.ShapeDtypeStruct((width * SHARE, width), jnp.bfloat16),
        scratch_shapes=[pltpu.VMEM((width * SHARE, width), jnp.float32)],
        name="shares",
    )(*sums)


def conv_rows(pad_ref, tap_ref, row0, row_count, cols):
    out = {}
    for s in range(0, cols, 8):
        sums = [jnp.zeros((8, 128), jnp.float32) for _ in range(row_count)]
        for b in range(TAPS):
            taps = [tap_ref[(TAPS - 1 - a) * TAPS + TAPS - 1 - b] for a in range(TAPS)]
            for reached in range(row_count + TAPS - 1):
                start = OFF - REACH + b + s
                cells = pad_ref[row0 + reached, start : start + 8, :]
                for a in range(TAPS):
                    if 0 <= reached - a < row_count:
                        sums[reached - a] = sums[reached - a] + cells * taps[a]
        for r in range(row_count):
            out[r, s] = sums[r]
    return out


def spread_kernel(
    block_rows,
    own,
    top,
    bottom,
    left,
    right,
    cot_ref,
    kern_ref,
    out_ref,
    pad_ref,
    pair_ref,
    w_ref,
    tap_ref,
    cell_ref,
):
    step = pl.program_id(0)
    cols = own.shape[1]
    half = cols // 2
    upper = block_rows - VECTOR_ROWS
    count = upper * half

    @pl.when(step == 0)
    def _():
        fill_weights(kern_ref, w_ref, True)
        fill_padded(own, top, bottom, left, right, pad_ref)
        fill_pairs(pad_ref, pair_ref)
        for a in range(TAPS):
            for b in range(TAPS):
                tap_ref[a * TAPS + b] = jnp.broadcast_to(kern_ref[a, b : b + 1, :], (8, 128))

    @pl.when(step < pl.num_programs(0))
    def _():
        rows = conv_rows(pad_ref, tap_ref, step * block_rows + upper, VECTOR_ROWS, cols)
        conv = conv_pairs(pair_ref, w_ref, step * block_rows, upper, half)
        for q in range(2):
            cell_ref[pl.ds(q, count, stride=2), :] = conv[:, q * 128 : q * 128 + 128]
        for (r, s), value in rows.items():
            at = (upper + r) * cols + s
            cell_ref[at : at + 8, :] = value
        out_ref[...] = (cell_ref[...] + cot_ref[...].astype(jnp.float32)).astype(jnp.bfloat16)


def spread(dconv, sides, cotangent, kernel):
    rows, cols, width = dconv.shape
    block_rows = 16
    block = block_rows * cols
    padded = rows + 2 * REACH
    whole = lambda a: pl.BlockSpec(a.shape, lambda i: (0,) * a.ndim)
    cells = pl.BlockSpec((block, width), lambda i: (i, 0))
    return pl.pallas_call(
        functools.partial(spread_kernel, block_rows),
        grid=(rows // block_rows,),
        in_specs=[whole(dconv)] + [whole(s) for s in sides] + [cells, whole(kernel)],
        out_specs=cells,
        out_shape=jax.ShapeDtypeStruct((rows * cols, width), jnp.bfloat16),
        scratch_shapes=[
            pltpu.VMEM((padded, cols + 2 * OFF, width), jnp.float32),
            pltpu.VMEM((PAIRS, padded * cols // 2, 2 * width), jnp.bfloat16),
            pltpu.VMEM((TAPS * PAIRS * 2 * width, 2 * width), jnp.bfloat16),
            pltpu.VMEM((TAPS * TAPS, 8, width), jnp.float32),
            pltpu.VMEM((block, width), jnp.float32),
        ],
        compiler_params=pltpu.CompilerParams(vmem_limit_bytes=GRANT),
        name="spread",
    )(dconv, *sides, cotangent.reshape(rows * cols, width), kernel).reshape(rows, cols, width)


def total(parts):
    axes = ("gx", "gy")
    share = lax.all_to_all(parts, axes, split_axis=0, concat_axis=0, tiled=True)
    share = jnp.sum(share.astype(jnp.float32), axis=0).astype(parts.dtype)
    copies = jnp.broadcast_to(share[None], parts.shape)
    return lax.all_to_all(copies, axes, split_axis=0, concat_axis=0, tiled=True)


def finish_kernel(
    factor,
    summed_ref,
    wdown_ref,
    bdown_ref,
    scale_ref,
    dkern_ref,
    dkbias_ref,
    dgain_ref,
    dshift_ref,
    dwup_ref,
    dbup_ref,
    dwdown_ref,
    dbdown_ref,
    dscale_ref,
    stage_ref,
):
    stage_ref[...] = summed_ref[...].astype(jnp.float32) * factor
    scale = scale_ref[...]

    def small(i):
        at = i * SHARE + 2 * LANES
        return stage_ref[at : at + 1, :]

    for a in range(TAPS):
        for b in range(TAPS):
            dkern_ref[a, b : b + 1, :] = small(a * TAPS + b)
    first = TAPS * TAPS
    dkbias_ref[...] = small(first)
    dgain_ref[...] = small(first + 1)
    dshift_ref[...] = small(first + 2)
    cot_sum = small(first + 3)
    dscale = bdown_ref[...] * cot_sum
    for k in range(LANES):
        lanes = slice(k * 128, k * 128 + 128)
        dbup_ref[:, lanes] = small(first + 4 + k)
        dwup_ref[:, lanes] = stage_ref[pl.ds(k, 128, stride=SHARE), :]
        product = stage_ref[pl.ds(LANES + k, 128, stride=SHARE), :].T
        dwdown_ref[lanes, :] = product * scale
        weights = wdown_ref[lanes, :].astype(jnp.float32)
        dscale = dscale + jnp.sum(product * weights, axis=0, keepdims=True)
    dbdown_ref[...] = cot_sum * scale
    dscale_ref[...] = dscale


def finish(summed, w_down, b_down, layer_scale, factor):
    hidden, width = w_down.shape
    shapes = [(TAPS, TAPS, width)] + [(1, width)] * 3 + [(width, hidden), (1, hidden), (hidden, width)]
    shapes += [(1, width)] * 2
    row = lambda a: a.reshape(1, -1)
    return pl.pallas_call(
        functools.partial(finish_kernel, factor),
        out_shape=[jax.ShapeDtypeStruct(shape, jnp.float32) for shape in shapes],
        scratch_shapes=[pltpu.VMEM(summed.shape, jnp.float32)],
        name="finish",
    )(summed, w_down, row(b_down), row(layer_scale))


def local(
    features, cotangent, kernel, kernel_bias, norm_gain, norm_shift, w_up, b_up, w_down, b_down, layer_scale
):
    rows, cols, width = features.shape
    devices = lax.axis_size("gx") * lax.axis_size("gy")
    dconv, *sums = layer(
        features,
        halo(features),
        cotangent,
        kernel,
        kernel_bias,
        norm_gain,
        norm_shift,
        w_up,
        b_up,
        w_down,
        layer_scale,
    )
    dconv = dconv.reshape(rows, cols, width)
    d_features = spread(dconv, halo(dconv), cotangent, kernel)
    summed = total(shares(*sums).reshape(devices, SHARE, width)).reshape(devices * SHARE, width)
    factor = 1.0 / math.sqrt(rows * cols * devices)
    grads = finish(summed, w_down, b_down, layer_scale, factor)
    return (d_features,) + tuple(g.reshape(-1) if g.shape[0] == 1 else g for g in grads)


def solution(mesh):
    placed = (P("gx", "gy", None), P("gx", "gy", None), P(), P(), P(), P(), P(), P(), P(), P(), P())
    return jax.shard_map(
        local,
        mesh=mesh,
        in_specs=placed,
        out_specs=(P("gx", "gy", None), P(), P(), P(), P(), P(), P(), P(), P(), P()),
        check_vma=False,
    )
```

```python
import functools
import math

import jax
import jax.numpy as jnp
from jax import lax
from jax.experimental import pallas as pl
from jax.experimental.pallas import tpu as pltpu
from jax.sharding import PartitionSpec as P


EPSILON = 1e-06
REACH = 3
TAPS = 7
PAIRS = 4
OFF = 8
GRANT = 58 * 2**20
VECTOR_ROWS = 8
LANES = 4
SHARE = 16


def shifted(cells, axis, step, cyclic):
    count = lax.axis_size(axis)
    pairs = [(i, (i + step) % count) for i in range(count) if cyclic or 0 <= i + step < count]
    return lax.ppermute(cells, axis, pairs)


def halo(cells):
    rows, cols = cells.shape[0], cells.shape[1]
    top = shifted(cells[rows - REACH :], "gx", 1, True)
    bottom = shifted(cells[:REACH], "gx", -1, True)

    def edge(start):
        cut = [part[:, start : start + REACH] for part in (top, cells, bottom)]
        return jnp.concatenate(cut, axis=0)

    ends = edge(cols - REACH), edge(0)
    left = shifted(ends[0], "gy", 1, False)
    right = shifted(ends[1], "gy", -1, False)
    return top, bottom, left, right


def fill_padded(own, top, bottom, left, right, pad_ref):
    rows, cols = own.shape[0], own.shape[1]
    inner = pl.ds(OFF, cols)
    pad_ref[0:REACH, inner, :] = top[...].astype(jnp.float32)
    pad_ref[REACH + rows : 2 * REACH + rows, inner, :] = bottom[...].astype(jnp.float32)

    def body(r, carry):
        pad_ref[REACH + r, inner, :] = own[r].astype(jnp.float32)
        return carry

    lax.fori_loop(0, rows, body, 0, unroll=4)

    def sides(r, carry):
        pad_ref[r, OFF - REACH : OFF, :] = left[r].astype(jnp.float32)
        pad_ref[r, OFF + cols : OFF + cols + REACH, :] = right[r].astype(jnp.float32)
        return carry

    lax.fori_loop(0, rows + 2 * REACH, sides, 0, unroll=2)


def fill_pairs(pad_ref, pair_ref):
    half = pair_ref.shape[1] // pad_ref.shape[0]

    def body(r, carry):
        for m in range(PAIRS):
            for p in range(2):
                start = OFF - REACH + 2 * m + p
                cells = pad_ref[r, pl.ds(start, half, stride=2), :]
                pair_ref[m, pl.ds(pl.multiple_of(r * half, half), half), p * 128 : p * 128 + 128] = (
                    cells.astype(jnp.bfloat16)
                )
        return carry

    lax.fori_loop(0, pad_ref.shape[0], body, 0, unroll=2)


def fill_weights(kern_ref, w_ref, flip):
    width = kern_ref.shape[2]
    row = lax.broadcasted_iota(jnp.int32, (width, width), 0)
    col = lax.broadcasted_iota(jnp.int32, (width, width), 1)
    eye = row == col
    for a in range(TAPS):
        for m in range(PAIRS):
            for p in range(2):
                for q in range(2):
                    b = 2 * m + p - q
                    base = ((a * PAIRS + m) * 2 + p) * width
                    if 0 <= b < TAPS:
                        tap = (
                            kern_ref[TAPS - 1 - a, pl.ds(TAPS - 1 - b, 1), :]
                            if flip
                            else kern_ref[a, pl.ds(b, 1), :]
                        )
                        block = jnp.where(eye, jnp.broadcast_to(tap, (width, width)), 0.0)
                    else:
                        block = jnp.zeros((width, width), jnp.float32)
                    w_ref[base : base + width, q * width : (q + 1) * width] = block.astype(
                        jnp.bfloat16
                    )


def conv_pairs(pair_ref, w_ref, row0, row_count, half):
    lhs = jnp.concatenate(
        [
            pair_ref[m, pl.ds(pl.multiple_of((row0 + a) * half, half), row_count * half), :]
            for a in range(TAPS)
            for m in range(PAIRS)
        ],
        axis=1,
    )
    return jnp.dot(lhs, w_ref[...], preferred_element_type=jnp.float32)


def dot(left, right, dims):
    return lax.dot_general(left, right, (dims, ((), ())), preferred_element_type=jnp.float32)


def fold(values):
    return jnp.sum(values.reshape(-1, 8, values.shape[-1]), axis=0)


def tap_sums(pad_ref, cell_ref, row0, row_count, cols):
    sums = {}
    for b in range(TAPS):
        for a in range(TAPS):
            sums[a, b] = jnp.zeros((8, 128), jnp.float32)
        for s in range(0, cols, 8):
            grads = [cell_ref[r * cols + s : r * cols + s + 8, :] for r in range(row_count)]
            for reached in range(row_count + TAPS - 1):
                start = OFF - REACH + b + s
                cells = pad_ref[row0 + reached, start : start + 8, :]
                for a in range(TAPS):
                    if 0 <= reached - a < row_count:
                        sums[a, b] = sums[a, b] + cells * grads[reached - a]
    return sums


def layer_kernel(
    block_rows,
    own,
    top,
    bottom,
    left,
    right,
    cot_ref,
    kern_ref,
    kbias_ref,
    gain_ref,
    shift_ref,
    wup_ref,
    bup_ref,
    wdown_ref,
    scale_ref,
    dconv_ref,
    dwup_ref,
    dgt_ref,
    sums_ref,
    dbup_ref,
    dkern_ref,
    pad_ref,
    pair_ref,
    w_ref,
    cell_ref,
    conv_ref,
):
    step = pl.program_id(0)
    cols = own.shape[1]
    half = cols // 2
    count = block_rows * half

    @pl.when(step == 0)
    def _():
        fill_weights(kern_ref, w_ref, False)
        fill_padded(own, top, bottom, left, right, pad_ref)
        fill_pairs(pad_ref, pair_ref)
        dwup_ref[...] = jnp.zeros_like(dwup_ref)
        dgt_ref[...] = jnp.zeros_like(dgt_ref)
        sums_ref[...] = jnp.zeros_like(sums_ref)
        dbup_ref[...] = jnp.zeros_like(dbup_ref)
        dkern_ref[...] = jnp.zeros_like(dkern_ref)
        conv_ref[...] = conv_pairs(pair_ref, w_ref, 0, block_rows, half)

    conv = conv_ref[...]
    conv = jnp.concatenate([conv[:, :128], conv[:, 128:]], axis=0) + kbias_ref[...]
    gain = gain_ref[...]
    centred = conv - jnp.mean(conv, axis=-1, keepdims=True)
    inv_std = lax.rsqrt(jnp.mean(centred * centred, axis=-1, keepdims=True) + EPSILON)
    normed = centred * inv_std
    normal = (normed * gain + shift_ref[...]).astype(jnp.bfloat16)
    hidden = dot(normal, wup_ref[...], ((1,), (0,))) + bup_ref[...]
    cdf = 0.5 * (1.0 + lax.erf(hidden * 0.7071067811865476))
    active = (hidden * cdf).astype(jnp.bfloat16)
    slope = cdf + hidden * jnp.exp(-0.5 * hidden * hidden) * 0.3989422804014327
    cell_ref[...] = cot_ref[...].astype(jnp.float32)
    cot = jnp.concatenate([cell_ref[pl.ds(q, count, stride=2), :] for q in range(2)], axis=0)
    d_output = (cot * scale_ref[...]).astype(jnp.bfloat16)
    d_hidden = (dot(d_output, wdown_ref[...], ((1,), (1,))) * slope).astype(jnp.bfloat16)
    d_normal = dot(d_hidden, wup_ref[...], ((1,), (1,)))
    d_normed = d_normal * gain
    first = jnp.mean(d_normed, axis=-1, keepdims=True)
    second = jnp.mean(d_normed * normed, axis=-1, keepdims=True)
    d_conv = inv_std * (d_normed - first - normed * second)
    sums_ref[0] += fold(d_conv)
    sums_ref[1] += fold(d_normal * normed)
    sums_ref[2] += fold(d_normal)
    sums_ref[3] += fold(cot)
    dbup_ref[...] += fold(d_hidden.astype(jnp.float32))
    dwup_ref[...] += dot(normal, d_hidden, ((0,), (0,)))
    dgt_ref[...] += dot(cot.astype(jnp.bfloat16), active, ((0,), (0,)))
    for q in range(2):
        cell_ref[pl.ds(q, count, stride=2), :] = d_conv[q * count : (q + 1) * count]
    dconv_ref[...] = cell_ref[...].astype(jnp.bfloat16)

    @pl.when(step < pl.num_programs(0))
    def _():
        following = jnp.minimum(step + 1, pl.num_programs(0) - 1)
        taps = tap_sums(pad_ref, cell_ref, step * block_rows, block_rows, cols)
        conv = conv_pairs(pair_ref, w_ref, following * block_rows, block_rows, half)
        conv_ref[...] = conv
        for (a, b), value in taps.items():
            dkern_ref[a, b] += value


def layer(x, sides, cotangent, kernel, kbias, gain, shift, wup, bup, wdown, scale):
    rows, cols, width = x.shape
    hidden = wup.shape[1]
    block_rows = 16
    block = block_rows * cols
    whole = lambda a: pl.BlockSpec(a.shape, lambda i: (0,) * a.ndim)
    row = lambda a: a.reshape(1, -1)
    consts = (kernel, row(kbias), row(gain), row(shift), wup, row(bup), wdown, row(scale))
    padded = rows + 2 * REACH
    cells = pl.BlockSpec((block, width), lambda i: (i, 0))
    full = lambda *shape: pl.BlockSpec(shape, lambda i: (0,) * len(shape))
    f32 = jnp.float32
    return pl.pallas_call(
        functools.partial(layer_kernel, block_rows),
        grid=(rows // block_rows,),
        in_specs=[whole(x)]
        + [whole(s) for s in sides]
        + [cells]
        + [whole(c) for c in consts],
        out_specs=[
            cells,
            full(width, hidden),
            full(width, hidden),
            full(4, 8, width),
            full(8, hidden),
            full(TAPS, TAPS, 8, width),
        ],
        out_shape=[
            jax.ShapeDtypeStruct((rows * cols, width), jnp.bfloat16),
            jax.ShapeDtypeStruct((width, hidden), f32),
            jax.ShapeDtypeStruct((width, hidden), f32),
            jax.ShapeDtypeStruct((4, 8, width), f32),
            jax.ShapeDtypeStruct((8, hidden), f32),
            jax.ShapeDtypeStruct((TAPS, TAPS, 8, width), f32),
        ],
        scratch_shapes=[
            pltpu.VMEM((padded, cols + 2 * OFF, width), f32),
            pltpu.VMEM((PAIRS, padded * cols // 2, 2 * width), jnp.bfloat16),
            pltpu.VMEM((TAPS * PAIRS * 2 * width, 2 * width), jnp.bfloat16),
            pltpu.VMEM((block, width), f32),
            pltpu.VMEM((block // 2, 2 * width), f32),
        ],
        compiler_params=pltpu.CompilerParams(vmem_limit_bytes=GRANT),
        name="layer",
    )(x, *sides, cotangent.reshape(rows * cols, width), *consts)


def parts_kernel(dwup_ref, dgt_ref, sums_ref, dbup_ref, dkern_ref, parts_ref, stage_ref):
    stage_ref[...] = jnp.zeros_like(stage_ref)
    for k in range(LANES):
        lanes = slice(k * 128, k * 128 + 128)
        stage_ref[pl.ds(k, 128, stride=SHARE), :] = dwup_ref[:, lanes]
        stage_ref[pl.ds(LANES + k, 128, stride=SHARE), :] = dgt_ref[:, lanes]
    small = [dkern_ref[a, b] for a in range(TAPS) for b in range(TAPS)]
    small += [sums_ref[k] for k in range(4)]
    small += [dbup_ref[:, k * 128 : k * 128 + 128] for k in range(LANES)]
    for i, value in enumerate(small):
        at = i * SHARE + 2 * LANES
        stage_ref[at : at + 1, :] = jnp.sum(value, axis=0, keepdims=True)
    parts_ref[...] = stage_ref[...].astype(jnp.bfloat16)


def shares(*sums):
    width = sums[0].shape[0]
    return pl.pallas_call(
        parts_kernel,
        out_shape=jax.ShapeDtypeStruct((width * SHARE, width), jnp.bfloat16),
        scratch_shapes=[pltpu.VMEM((width * SHARE, width), jnp.float32)],
        name="shares",
    )(*sums)


def conv_rows(pad_ref, tap_ref, row0, row_count, cols):
    out = {}
    for s in range(0, cols, 8):
        sums = [jnp.zeros((8, 128), jnp.float32) for _ in range(row_count)]
        for b in range(TAPS):
            taps = [tap_ref[(TAPS - 1 - a) * TAPS + TAPS - 1 - b] for a in range(TAPS)]
            for reached in range(row_count + TAPS - 1):
                start = OFF - REACH + b + s
                cells = pad_ref[row0 + reached, start : start + 8, :]
                for a in range(TAPS):
                    if 0 <= reached - a < row_count:
                        sums[reached - a] = sums[reached - a] + cells * taps[a]
        for r in range(row_count):
            out[r, s] = sums[r]
    return out


def spread_kernel(
    block_rows,
    own,
    top,
    bottom,
    left,
    right,
    cot_ref,
    kern_ref,
    out_ref,
    pad_ref,
    pair_ref,
    w_ref,
    tap_ref,
    cell_ref,
):
    step = pl.program_id(0)
    cols = own.shape[1]
    half = cols // 2
    upper = block_rows - VECTOR_ROWS
    count = upper * half

    @pl.when(step == 0)
    def _():
        fill_weights(kern_ref, w_ref, True)
        fill_padded(own, top, bottom, left, right, pad_ref)
        fill_pairs(pad_ref, pair_ref)
        for a in range(TAPS):
            for b in range(TAPS):
                tap_ref[a * TAPS + b] = jnp.broadcast_to(kern_ref[a, b : b + 1, :], (8, 128))

    @pl.when(step < pl.num_programs(0))
    def _():
        rows = conv_rows(pad_ref, tap_ref, step * block_rows + upper, VECTOR_ROWS, cols)
        conv = conv_pairs(pair_ref, w_ref, step * block_rows, upper, half)
        for q in range(2):
            cell_ref[pl.ds(q, count, stride=2), :] = conv[:, q * 128 : q * 128 + 128]
        for (r, s), value in rows.items():
            at = (upper + r) * cols + s
            cell_ref[at : at + 8, :] = value
        out_ref[...] = (cell_ref[...] + cot_ref[...].astype(jnp.float32)).astype(jnp.bfloat16)


def spread(dconv, sides, cotangent, kernel):
    rows, cols, width = dconv.shape
    block_rows = 16
    block = block_rows * cols
    padded = rows + 2 * REACH
    whole = lambda a: pl.BlockSpec(a.shape, lambda i: (0,) * a.ndim)
    cells = pl.BlockSpec((block, width), lambda i: (i, 0))
    return pl.pallas_call(
        functools.partial(spread_kernel, block_rows),
        grid=(rows // block_rows,),
        in_specs=[whole(dconv)] + [whole(s) for s in sides] + [cells, whole(kernel)],
        out_specs=cells,
        out_shape=jax.ShapeDtypeStruct((rows * cols, width), jnp.bfloat16),
        scratch_shapes=[
            pltpu.VMEM((padded, cols + 2 * OFF, width), jnp.float32),
            pltpu.VMEM((PAIRS, padded * cols // 2, 2 * width), jnp.bfloat16),
            pltpu.VMEM((TAPS * PAIRS * 2 * width, 2 * width), jnp.bfloat16),
            pltpu.VMEM((TAPS * TAPS, 8, width), jnp.float32),
            pltpu.VMEM((block, width), jnp.float32),
        ],
        compiler_params=pltpu.CompilerParams(vmem_limit_bytes=GRANT),
        name="spread",
    )(dconv, *sides, cotangent.reshape(rows * cols, width), kernel).reshape(rows, cols, width)


def total(parts):
    axes = ("gx", "gy")
    share = lax.all_to_all(parts, axes, split_axis=0, concat_axis=0, tiled=True)
    share = jnp.sum(share.astype(jnp.float32), axis=0).astype(parts.dtype)
    copies = jnp.broadcast_to(share[None], parts.shape)
    return lax.all_to_all(copies, axes, split_axis=0, concat_axis=0, tiled=True)


def finish_kernel(
    factor,
    summed_ref,
    wdown_ref,
    bdown_ref,
    scale_ref,
    dkern_ref,
    dkbias_ref,
    dgain_ref,
    dshift_ref,
    dwup_ref,
    dbup_ref,
    dwdown_ref,
    dbdown_ref,
    dscale_ref,
    stage_ref,
):
    stage_ref[...] = summed_ref[...].astype(jnp.float32) * factor
    scale = scale_ref[...]

    def small(i):
        at = i * SHARE + 2 * LANES
        return stage_ref[at : at + 1, :]

    for a in range(TAPS):
        for b in range(TAPS):
            dkern_ref[a, b : b + 1, :] = small(a * TAPS + b)
    first = TAPS * TAPS
    dkbias_ref[...] = small(first)
    dgain_ref[...] = small(first + 1)
    dshift_ref[...] = small(first + 2)
    cot_sum = small(first + 3)
    dscale = bdown_ref[...] * cot_sum
    for k in range(LANES):
        lanes = slice(k * 128, k * 128 + 128)
        dbup_ref[:, lanes] = small(first + 4 + k)
        dwup_ref[:, lanes] = stage_ref[pl.ds(k, 128, stride=SHARE), :]
        product = stage_ref[pl.ds(LANES + k, 128, stride=SHARE), :].T
        dwdown_ref[lanes, :] = product * scale
        weights = wdown_ref[lanes, :].astype(jnp.float32)
        dscale = dscale + jnp.sum(product * weights, axis=0, keepdims=True)
    dbdown_ref[...] = cot_sum * scale
    dscale_ref[...] = dscale


def finish(summed, w_down, b_down, layer_scale, factor):
    hidden, width = w_down.shape
    shapes = [(TAPS, TAPS, width)] + [(1, width)] * 3 + [(width, hidden), (1, hidden), (hidden, width)]
    shapes += [(1, width)] * 2
    row = lambda a: a.reshape(1, -1)
    return pl.pallas_call(
        functools.partial(finish_kernel, factor),
        out_shape=[jax.ShapeDtypeStruct(shape, jnp.float32) for shape in shapes],
        scratch_shapes=[pltpu.VMEM(summed.shape, jnp.float32)],
        name="finish",
    )(summed, w_down, row(b_down), row(layer_scale))


def local(
    features, cotangent, kernel, kernel_bias, norm_gain, norm_shift, w_up, b_up, w_down, b_down, layer_scale
):
    rows, cols, width = features.shape
    devices = lax.axis_size("gx") * lax.axis_size("gy")
    dconv, *sums = layer(
        features,
        halo(features),
        cotangent,
        kernel,
        kernel_bias,
        norm_gain,
        norm_shift,
        w_up,
        b_up,
        w_down,
        layer_scale,
    )
    dconv = dconv.reshape(rows, cols, width)
    d_features = spread(dconv, halo(dconv), cotangent, kernel)
    parts = shares(*sums)
    summed = total(parts.reshape(devices, SHARE, width)).reshape(devices * SHARE, width)
    factor = 1.0 / math.sqrt(rows * cols * devices)
    grads = finish(summed, w_down, b_down, layer_scale, factor)
    return (d_features,) + tuple(g.reshape(-1) if g.shape[0] == 1 else g for g in grads)


def solution(mesh):
    placed = (P("gx", "gy", None), P("gx", "gy", None), P(), P(), P(), P(), P(), P(), P(), P(), P())
    return jax.shard_map(
        local,
        mesh=mesh,
        in_specs=placed,
        out_specs=(P("gx", "gy", None), P(), P(), P(), P(), P(), P(), P(), P(), P()),
        check_vma=False,
    )
```

```python
import functools
import math

import jax
import jax.numpy as jnp
from jax import lax
from jax.experimental import pallas as pl
from jax.experimental.pallas import tpu as pltpu
from jax.sharding import PartitionSpec as P


EPSILON = 1e-06
REACH = 3
TAPS = 7
PAIRS = 4
OFF = 8
GRANT = 58 * 2**20
VECTOR_ROWS = 8
LANES = 4
SHARE = 16


def shifted(cells, axis, step, cyclic):
    count = lax.axis_size(axis)
    pairs = [(i, (i + step) % count) for i in range(count) if cyclic or 0 <= i + step < count]
    return lax.ppermute(cells, axis, pairs)


def halo(cells):
    rows, cols = cells.shape[0], cells.shape[1]
    top = shifted(cells[rows - REACH :], "gx", 1, True)
    bottom = shifted(cells[:REACH], "gx", -1, True)

    def edge(start):
        cut = [part[:, start : start + REACH] for part in (top, cells, bottom)]
        return jnp.concatenate(cut, axis=0)

    ends = edge(cols - REACH), edge(0)
    left = shifted(ends[0], "gy", 1, False)
    right = shifted(ends[1], "gy", -1, False)
    return top, bottom, left, right


def fill_padded(own, top, bottom, left, right, pad_ref):
    rows, cols = own.shape[0], own.shape[1]
    inner = pl.ds(OFF, cols)
    pad_ref[0:REACH, inner, :] = top[...].astype(jnp.float32)
    pad_ref[REACH + rows : 2 * REACH + rows, inner, :] = bottom[...].astype(jnp.float32)

    def body(r, carry):
        pad_ref[REACH + r, inner, :] = own[r].astype(jnp.float32)
        return carry

    lax.fori_loop(0, rows, body, 0, unroll=4)

    def sides(r, carry):
        pad_ref[r, OFF - REACH : OFF, :] = left[r].astype(jnp.float32)
        pad_ref[r, OFF + cols : OFF + cols + REACH, :] = right[r].astype(jnp.float32)
        return carry

    span = rows + 2 * REACH
    lax.fori_loop(0, span // 8, lambda i, carry: [sides(8 * i + k, carry) for k in range(8)][0], 0)
    for r in range(span // 8 * 8, span):
        sides(r, 0)


def fill_pairs(pad_ref, pair_ref):
    half = pair_ref.shape[1] // pad_ref.shape[0]

    def body(r, carry):
        for m in range(PAIRS):
            for p in range(2):
                start = OFF - REACH + 2 * m + p
                cells = pad_ref[r, pl.ds(start, half, stride=2), :]
                pair_ref[m, pl.ds(pl.multiple_of(r * half, half), half), p * 128 : p * 128 + 128] = (
                    cells.astype(jnp.bfloat16)
                )
        return carry

    count = pad_ref.shape[0]
    lax.fori_loop(0, count // 8, lambda i, carry: [body(8 * i + k, carry) for k in range(8)][0], 0)
    for r in range(count // 8 * 8, count):
        body(r, 0)


def fill_weights(kern_ref, w_ref, flip):
    width = kern_ref.shape[2]
    row = lax.broadcasted_iota(jnp.int32, (width, width), 0)
    col = lax.broadcasted_iota(jnp.int32, (width, width), 1)
    eye = row == col
    for a in range(TAPS):
        for m in range(PAIRS):
            for p in range(2):
                for q in range(2):
                    b = 2 * m + p - q
                    base = ((a * PAIRS + m) * 2 + p) * width
                    if 0 <= b < TAPS:
                        tap = (
                            kern_ref[TAPS - 1 - a, pl.ds(TAPS - 1 - b, 1), :]
                            if flip
                            else kern_ref[a, pl.ds(b, 1), :]
                        )
                        block = jnp.where(eye, jnp.broadcast_to(tap, (width, width)), 0.0)
                    else:
                        block = jnp.zeros((width, width), jnp.float32)
                    w_ref[base : base + width, q * width : (q + 1) * width] = block.astype(
                        jnp.bfloat16
                    )


def conv_pairs(pair_ref, w_ref, row0, row_count, half):
    lhs = jnp.concatenate(
        [
            pair_ref[m, pl.ds(pl.multiple_of((row0 + a) * half, half), row_count * half), :]
            for a in range(TAPS)
            for m in range(PAIRS)
        ],
        axis=1,
    )
    return jnp.dot(lhs, w_ref[...], preferred_element_type=jnp.float32)


def dot(left, right, dims):
    return lax.dot_general(left, right, (dims, ((), ())), preferred_element_type=jnp.float32)


def fold(values):
    return jnp.sum(values.reshape(-1, 8, values.shape[-1]), axis=0)


def tap_sums(pad_ref, cell_ref, row0, row_count, cols):
    sums = {}
    for b in range(TAPS):
        for a in range(TAPS):
            sums[a, b] = jnp.zeros((8, 128), jnp.float32)
        for s in range(0, cols, 8):
            grads = [cell_ref[r * cols + s : r * cols + s + 8, :] for r in range(row_count)]
            for reached in range(row_count + TAPS - 1):
                start = OFF - REACH + b + s
                cells = pad_ref[row0 + reached, start : start + 8, :]
                for a in range(TAPS):
                    if 0 <= reached - a < row_count:
                        sums[a, b] = sums[a, b] + cells * grads[reached - a]
    return sums


def layer_kernel(
    block_rows,
    own,
    top,
    bottom,
    left,
    right,
    cot_ref,
    kern_ref,
    kbias_ref,
    gain_ref,
    shift_ref,
    wup_ref,
    bup_ref,
    wdown_ref,
    scale_ref,
    dconv_ref,
    dwup_ref,
    dgt_ref,
    sums_ref,
    dbup_ref,
    dkern_ref,
    pad_ref,
    pair_ref,
    w_ref,
    cell_ref,
    conv_ref,
):
    step = pl.program_id(0)
    cols = own.shape[1]
    half = cols // 2
    count = block_rows * half

    @pl.when(step == 0)
    def _():
        fill_weights(kern_ref, w_ref, False)
        fill_padded(own, top, bottom, left, right, pad_ref)
        fill_pairs(pad_ref, pair_ref)
        dwup_ref[...] = jnp.zeros_like(dwup_ref)
        dgt_ref[...] = jnp.zeros_like(dgt_ref)
        sums_ref[...] = jnp.zeros_like(sums_ref)
        dbup_ref[...] = jnp.zeros_like(dbup_ref)
        dkern_ref[...] = jnp.zeros_like(dkern_ref)
        conv_ref[...] = conv_pairs(pair_ref, w_ref, 0, block_rows, half)

    conv = conv_ref[...]
    conv = jnp.concatenate([conv[:, :128], conv[:, 128:]], axis=0) + kbias_ref[...]
    gain = gain_ref[...]
    centred = conv - jnp.mean(conv, axis=-1, keepdims=True)
    inv_std = lax.rsqrt(jnp.mean(centred * centred, axis=-1, keepdims=True) + EPSILON)
    normed = centred * inv_std
    normal = (normed * gain + shift_ref[...]).astype(jnp.bfloat16)
    hidden = dot(normal, wup_ref[...], ((1,), (0,))) + bup_ref[...]
    cdf = 0.5 * (1.0 + lax.erf(hidden * 0.7071067811865476))
    active = (hidden * cdf).astype(jnp.bfloat16)
    slope = cdf + hidden * jnp.exp(-0.5 * hidden * hidden) * 0.3989422804014327
    cell_ref[...] = cot_ref[...].astype(jnp.float32)
    cot = jnp.concatenate([cell_ref[pl.ds(q, count, stride=2), :] for q in range(2)], axis=0)
    d_output = (cot * scale_ref[...]).astype(jnp.bfloat16)
    d_wide = dot(d_output, wdown_ref[...], ((1,), (1,))) * slope
    d_hidden = d_wide.astype(jnp.bfloat16)
    d_normal = dot(d_hidden, wup_ref[...], ((1,), (1,)))
    d_normed = d_normal * gain
    first = jnp.mean(d_normed, axis=-1, keepdims=True)
    second = jnp.mean(d_normed * normed, axis=-1, keepdims=True)
    d_conv = inv_std * (d_normed - first - normed * second)
    sums_ref[0] += fold(d_conv)
    sums_ref[1] += fold(d_normal * normed)
    sums_ref[2] += fold(d_normal)
    sums_ref[3] += fold(cot)
    dbup_ref[...] += fold(d_wide)
    dwup_ref[...] += dot(normal, d_hidden, ((0,), (0,)))
    dgt_ref[...] += dot(cot.astype(jnp.bfloat16), active, ((0,), (0,)))
    for q in range(2):
        cell_ref[pl.ds(q, count, stride=2), :] = d_conv[q * count : (q + 1) * count]
    dconv_ref[...] = cell_ref[...].astype(jnp.bfloat16)

    @pl.when(step < pl.num_programs(0))
    def _():
        following = jnp.minimum(step + 1, pl.num_programs(0) - 1)
        taps = tap_sums(pad_ref, cell_ref, step * block_rows, block_rows, cols)
        conv = conv_pairs(pair_ref, w_ref, following * block_rows, block_rows, half)
        conv_ref[...] = conv
        for (a, b), value in taps.items():
            dkern_ref[a, b] += value


def layer(x, sides, cotangent, kernel, kbias, gain, shift, wup, bup, wdown, scale):
    rows, cols, width = x.shape
    hidden = wup.shape[1]
    block_rows = 16
    block = block_rows * cols
    whole = lambda a: pl.BlockSpec(a.shape, lambda i: (0,) * a.ndim)
    row = lambda a: a.reshape(1, -1)
    consts = (kernel, row(kbias), row(gain), row(shift), wup, row(bup), wdown, row(scale))
    padded = rows + 2 * REACH
    cells = pl.BlockSpec((block, width), lambda i: (i, 0))
    full = lambda *shape: pl.BlockSpec(shape, lambda i: (0,) * len(shape))
    f32 = jnp.float32
    return pl.pallas_call(
        functools.partial(layer_kernel, block_rows),
        grid=(rows // block_rows,),
        in_specs=[whole(x)]
        + [whole(s) for s in sides]
        + [cells]
        + [whole(c) for c in consts],
        out_specs=[
            cells,
            full(width, hidden),
            full(width, hidden),
            full(4, 8, width),
            full(8, hidden),
            full(TAPS, TAPS, 8, width),
        ],
        out_shape=[
            jax.ShapeDtypeStruct((rows * cols, width), jnp.bfloat16),
            jax.ShapeDtypeStruct((width, hidden), f32),
            jax.ShapeDtypeStruct((width, hidden), f32),
            jax.ShapeDtypeStruct((4, 8, width), f32),
            jax.ShapeDtypeStruct((8, hidden), f32),
            jax.ShapeDtypeStruct((TAPS, TAPS, 8, width), f32),
        ],
        scratch_shapes=[
            pltpu.VMEM((padded, cols + 2 * OFF, width), f32),
            pltpu.VMEM((PAIRS, padded * cols // 2, 2 * width), jnp.bfloat16),
            pltpu.VMEM((TAPS * PAIRS * 2 * width, 2 * width), jnp.bfloat16),
            pltpu.VMEM((block, width), f32),
            pltpu.VMEM((block // 2, 2 * width), f32),
        ],
        compiler_params=pltpu.CompilerParams(vmem_limit_bytes=GRANT),
        name="layer",
    )(x, *sides, cotangent.reshape(rows * cols, width), *consts)


def parts_kernel(dwup_ref, dgt_ref, sums_ref, dbup_ref, dkern_ref, parts_ref, stage_ref):
    stage_ref[...] = jnp.zeros_like(stage_ref)
    for k in range(LANES):
        lanes = slice(k * 128, k * 128 + 128)
        stage_ref[pl.ds(k, 128, stride=SHARE), :] = dwup_ref[:, lanes]
        stage_ref[pl.ds(LANES + k, 128, stride=SHARE), :] = dgt_ref[:, lanes]
    small = [dkern_ref[a, b] for a in range(TAPS) for b in range(TAPS)]
    small += [sums_ref[k] for k in range(4)]
    small += [dbup_ref[:, k * 128 : k * 128 + 128] for k in range(LANES)]
    for i, value in enumerate(small):
        at = i * SHARE + 2 * LANES
        stage_ref[at : at + 1, :] = jnp.sum(value, axis=0, keepdims=True)
    parts_ref[...] = stage_ref[...].astype(jnp.bfloat16)


def shares(*sums):
    width = sums[0].shape[0]
    return pl.pallas_call(
        parts_kernel,
        out_shape=jax.ShapeDtypeStruct((width * SHARE, width), jnp.bfloat16),
        scratch_shapes=[pltpu.VMEM((width * SHARE, width), jnp.float32)],
        name="shares",
    )(*sums)


def conv_rows(pad_ref, tap_ref, row0, row_count, cols):
    out = {}
    for s in range(0, cols, 8):
        sums = [jnp.zeros((8, 128), jnp.float32) for _ in range(row_count)]
        for b in range(TAPS):
            taps = [tap_ref[(TAPS - 1 - a) * TAPS + TAPS - 1 - b] for a in range(TAPS)]
            for reached in range(row_count + TAPS - 1):
                start = OFF - REACH + b + s
                cells = pad_ref[row0 + reached, start : start + 8, :]
                for a in range(TAPS):
                    if 0 <= reached - a < row_count:
                        sums[reached - a] = sums[reached - a] + cells * taps[a]
        for r in range(row_count):
            out[r, s] = sums[r]
    return out


def spread_kernel(
    block_rows,
    own,
    top,
    bottom,
    left,
    right,
    cot_ref,
    kern_ref,
    out_ref,
    pad_ref,
    pair_ref,
    w_ref,
    tap_ref,
    cell_ref,
):
    step = pl.program_id(0)
    cols = own.shape[1]
    half = cols // 2
    upper = block_rows - VECTOR_ROWS
    count = upper * half

    @pl.when(step == 0)
    def _():
        fill_weights(kern_ref, w_ref, True)
        fill_padded(own, top, bottom, left, right, pad_ref)
        fill_pairs(pad_ref, pair_ref)
        for a in range(TAPS):
            for b in range(TAPS):
                tap_ref[a * TAPS + b] = jnp.broadcast_to(kern_ref[a, b : b + 1, :], (8, 128))

    @pl.when(step < pl.num_programs(0))
    def _():
        rows = conv_rows(pad_ref, tap_ref, step * block_rows + upper, VECTOR_ROWS, cols)
        conv = conv_pairs(pair_ref, w_ref, step * block_rows, upper, half)
        for q in range(2):
            cell_ref[pl.ds(q, count, stride=2), :] = conv[:, q * 128 : q * 128 + 128]
        for (r, s), value in rows.items():
            at = (upper + r) * cols + s
            cell_ref[at : at + 8, :] = value
        out_ref[...] = (cell_ref[...] + cot_ref[...].astype(jnp.float32)).astype(jnp.bfloat16)


def spread(dconv, sides, cotangent, kernel):
    rows, cols, width = dconv.shape
    block_rows = 16
    block = block_rows * cols
    padded = rows + 2 * REACH
    whole = lambda a: pl.BlockSpec(a.shape, lambda i: (0,) * a.ndim)
    cells = pl.BlockSpec((block, width), lambda i: (i, 0))
    return pl.pallas_call(
        functools.partial(spread_kernel, block_rows),
        grid=(rows // block_rows,),
        in_specs=[whole(dconv)] + [whole(s) for s in sides] + [cells, whole(kernel)],
        out_specs=cells,
        out_shape=jax.ShapeDtypeStruct((rows * cols, width), jnp.bfloat16),
        scratch_shapes=[
            pltpu.VMEM((padded, cols + 2 * OFF, width), jnp.float32),
            pltpu.VMEM((PAIRS, padded * cols // 2, 2 * width), jnp.bfloat16),
            pltpu.VMEM((TAPS * PAIRS * 2 * width, 2 * width), jnp.bfloat16),
            pltpu.VMEM((TAPS * TAPS, 8, width), jnp.float32),
            pltpu.VMEM((block, width), jnp.float32),
        ],
        compiler_params=pltpu.CompilerParams(vmem_limit_bytes=GRANT),
        name="spread",
    )(dconv, *sides, cotangent.reshape(rows * cols, width), kernel).reshape(rows, cols, width)


def total(parts):
    axes = ("gx", "gy")
    share = lax.all_to_all(parts, axes, split_axis=0, concat_axis=0, tiled=True)
    share = jnp.sum(share.astype(jnp.float32), axis=0).astype(parts.dtype)
    copies = jnp.broadcast_to(share[None], parts.shape)
    return lax.all_to_all(copies, axes, split_axis=0, concat_axis=0, tiled=True)


def finish_kernel(
    factor,
    summed_ref,
    wdown_ref,
    bdown_ref,
    scale_ref,
    dkern_ref,
    dkbias_ref,
    dgain_ref,
    dshift_ref,
    dwup_ref,
    dbup_ref,
    dwdown_ref,
    dbdown_ref,
    dscale_ref,
    stage_ref,
):
    stage_ref[...] = summed_ref[...].astype(jnp.float32) * factor
    scale = scale_ref[...]

    def small(i):
        at = i * SHARE + 2 * LANES
        return stage_ref[at : at + 1, :]

    for a in range(TAPS):
        for b in range(TAPS):
            dkern_ref[a, b : b + 1, :] = small(a * TAPS + b)
    first = TAPS * TAPS
    dkbias_ref[...] = small(first)
    dgain_ref[...] = small(first + 1)
    dshift_ref[...] = small(first + 2)
    cot_sum = small(first + 3)
    dscale = bdown_ref[...] * cot_sum
    for k in range(LANES):
        lanes = slice(k * 128, k * 128 + 128)
        dbup_ref[:, lanes] = small(first + 4 + k)
        dwup_ref[:, lanes] = stage_ref[pl.ds(k, 128, stride=SHARE), :]
        product = stage_ref[pl.ds(LANES + k, 128, stride=SHARE), :].T
        dwdown_ref[lanes, :] = product * scale
        weights = wdown_ref[lanes, :].astype(jnp.float32)
        dscale = dscale + jnp.sum(product * weights, axis=0, keepdims=True)
    dbdown_ref[...] = cot_sum * scale
    dscale_ref[...] = dscale


def finish(summed, w_down, b_down, layer_scale, factor):
    hidden, width = w_down.shape
    shapes = [(TAPS, TAPS, width)] + [(1, width)] * 3 + [(width, hidden), (1, hidden), (hidden, width)]
    shapes += [(1, width)] * 2
    row = lambda a: a.reshape(1, -1)
    return pl.pallas_call(
        functools.partial(finish_kernel, factor),
        out_shape=[jax.ShapeDtypeStruct(shape, jnp.float32) for shape in shapes],
        scratch_shapes=[pltpu.VMEM(summed.shape, jnp.float32)],
        name="finish",
    )(summed, w_down, row(b_down), row(layer_scale))


def local(
    features, cotangent, kernel, kernel_bias, norm_gain, norm_shift, w_up, b_up, w_down, b_down, layer_scale
):
    rows, cols, width = features.shape
    devices = lax.axis_size("gx") * lax.axis_size("gy")
    dconv, *sums = layer(
        features,
        halo(features),
        cotangent,
        kernel,
        kernel_bias,
        norm_gain,
        norm_shift,
        w_up,
        b_up,
        w_down,
        layer_scale,
    )
    dconv = dconv.reshape(rows, cols, width)
    d_features = spread(dconv, halo(dconv), cotangent, kernel)
    parts = shares(*sums)
    summed = total(parts.reshape(devices, SHARE, width)).reshape(devices * SHARE, width)
    factor = 1.0 / math.sqrt(rows * cols * devices)
    grads = finish(summed, w_down, b_down, layer_scale, factor)
    return (d_features,) + tuple(g.reshape(-1) if g.shape[0] == 1 else g for g in grads)


def solution(mesh):
    placed = (P("gx", "gy", None), P("gx", "gy", None), P(), P(), P(), P(), P(), P(), P(), P(), P())
    return jax.shard_map(
        local,
        mesh=mesh,
        in_specs=placed,
        out_specs=(P("gx", "gy", None), P(), P(), P(), P(), P(), P(), P(), P(), P()),
        check_vma=False,
    )
```
